32 devices in a mesh: role: 4 (over z), grp: 4 (over x, core), run: 2 (over y).
Axes of the slice: x: 2, y: 2, z: 4, core: 2. Of those that a mesh axis runs over, the one named last changes fastest.
Arguments:
- prior_fields: float32 [1024, 3, 32, 128], P(('role', 'grp'), None, 'run'), may hold values from -0.4 to 1.4, as said below
- measured_point_location: int32 [512], P('run'), may hold values from 0 to 2047
- measured_depths: float32 [512], P('run'), may hold values from 0.7 to 1.3
- inverse_noise_deviation: float32 [512], P('run'), may hold values from 5 to 40
- sample_noise_draw: float32 [1024, 512], P(None, 'run'), may hold values from -6 to 6
- sample_line_labels: int32 [1024], P(('role', 'grp')), may hold values from 0 to 1023, each once
Outputs:
- analysis: float32 [1024, 3, 32, 128], P(('role', 'grp'), None, 'run')
The draws below stay inside these ranges and needn't reach their ends.
Inputs may be any that keep to these rules, and one draw needn't show every extreme that they name: `prior_fields`: the depth component (index 0 of the second dimension) lies within 0.75 to 1.4, the momenta within -0.4 to 0.4.
All inputs are finite; a program needn't handle non-finite values.
Results may differ from the reference program's by a relative error of at most 0.0003.
Values sent between devices are 32-bit elements; how exact they have to be, the bound alone decides.
A program may use at most 64 MiB of HBM per device.

```python
import math
import jax
import jax.numpy as jnp
from jax import lax

ENSEMBLE_SIZE = 1024
POINTS_ACROSS = 128
RY = 16
OBS_DEV = 256
STEPS = 4
CHEB = 8
LATTICE_LINES = 32
NOBS = 512


def draw_prior_fields(key, part):
    keys = jax.random.split(jax.random.fold_in(key, 7), 2)
    depth = 1.0 + 0.25 * jax.random.uniform(keys[0], (ENSEMBLE_SIZE, 1, LATTICE_LINES, POINTS_ACROSS), jnp.float32, -1.0, 1.0)
    flows = jnp.clip(0.1 * jax.random.normal(keys[1], (ENSEMBLE_SIZE, 2, LATTICE_LINES, POINTS_ACROSS), jnp.float32), -0.4, 0.4)
    return jnp.concatenate([depth, flows], 1).astype(jnp.float32)


def touch_ends(values, key, least, high):
    extent = values.shape
    index_at = [jax.random.randint(jax.random.fold_in(key, axis), (), 0, extent[axis]) for axis in range(len(extent))]
    values = values.at[tuple(index_at)].set(least)
    longest = extent.index(max(extent))
    index_at[longest] = (index_at[longest] + 1) % extent[longest]
    return values.at[tuple(index_at)].set(high)


def shard_levels(rng, dims, cuts, low, high):
    def one(dim, shards_of):
        heights = jax.random.uniform(jax.random.fold_in(jax.random.fold_in(rng, 6), dim), (shards_of,), jnp.float32, low / len(cuts), high / len(cuts))
        return jnp.repeat(jnp.exp(heights), dims[dim] // shards_of).reshape((-1,) + (1,) * (len(dims) - dim - 1))

    factor_of = one(*cuts[0])
    for cut in cuts[1:]:
        factor_of = factor_of * one(*cut)
    return factor_of


def gaussian(own_key, shape, scale, most, cuts=(), kind=jnp.bfloat16):
    entries = jax.random.normal(own_key, shape, jnp.float32) * scale
    if len(cuts) > 0:
        entries = shard_levels(own_key, shape, cuts, -0.22, 0.18) * entries
    return jnp.clip(entries, min=-most, max=most).astype(kind)


def setup_inputs(seed: int = 0) -> dict:
    key_of = jax.random.split(jax.random.key(seed), 7)
    return {
        "prior_fields": draw_prior_fields(jax.random.fold_in(key_of[6], 71), 0),
        "measured_point_location": touch_ends(jax.random.randint(key_of[1], (NOBS,), 0, RY * POINTS_ACROSS), jax.random.fold_in(key_of[1], 1), 0, (RY * POINTS_ACROSS) - 1).astype(jnp.int32),
        "measured_depths": jnp.clip(0.7 + 0.59999996 * jax.random.uniform(key_of[2], (NOBS,), jnp.float32) ** shard_levels(key_of[2], (NOBS,), ((0, 2),), -0.2, 0.2), 0.7, 1.3),
        "inverse_noise_deviation": jnp.clip(jnp.exp(math.log(40.0) - 2.0794415 * jax.random.uniform(key_of[3], (NOBS,), jnp.float32) ** shard_levels(key_of[3], (NOBS,), ((0, 2),), -0.2, 0.2)), 5.0, 40.0),
        "sample_noise_draw": gaussian(key_of[4], (ENSEMBLE_SIZE, NOBS), 1.0, 6.0, ((1, 2),), jnp.float32),
        "sample_line_labels": jax.random.permutation(key_of[5], ENSEMBLE_SIZE).astype(jnp.int32),
    }


gravity = 1.0
courant = 0.35
widen_dispersion = 1.1

def lax_friedrichs(state):
    depth = state[:, 0]
    east = state[:, 1]
    north = state[:, 2]
    press = 0.5 * gravity * depth * depth
    flux_x = jnp.stack([east, east * east / depth + press, east * north / depth], 1)
    flux_y = jnp.stack([north, east * north / depth, north * north / depth + press], 1)
    inner = state[:, :, 1:-1]
    average = 0.25 * (state[:, :, 2:] + state[:, :, :-2] + jnp.roll(inner, 1, 3) + jnp.roll(inner, -1, 3))
    middle = flux_x[:, :, 1:-1]
    return average - 0.5 * courant * (jnp.roll(middle, -1, 3) - jnp.roll(middle, 1, 3)) - 0.5 * courant * (flux_y[:, :, 2:] - flux_y[:, :, :-2])

def prior_strip_slab(strip_slab):
    for step in range(STEPS):
        padded = jnp.concatenate([strip_slab[:, :, -1:], strip_slab, strip_slab[:, :, :1]], 2)
        strip_slab = lax_friedrichs(padded)
    return strip_slab

def reference(prior_fields, measured_point_location, measured_depths, inverse_noise_deviation, sample_noise_draw, sample_line_labels):
    propagated_fields = lax.map(prior_strip_slab, prior_fields.reshape(ENSEMBLE_SIZE // 16, 16, 3, LATTICE_LINES, POINTS_ACROSS)).reshape(ENSEMBLE_SIZE, 3, LATTICE_LINES, POINTS_ACROSS)
    blocks = (jnp.arange(NOBS, dtype=jnp.int32) // OBS_DEV).astype(jnp.int32)
    cells = (blocks * (RY * POINTS_ACROSS) + measured_point_location).astype(jnp.int32)
    depth_flat = propagated_fields[:, 0].reshape(ENSEMBLE_SIZE, LATTICE_LINES * POINTS_ACROSS)
    sampled = inverse_noise_deviation[None, :] * depth_flat[:, cells]
    innovation = inverse_noise_deviation[None, :] * measured_depths[None, :] - sampled + sample_noise_draw[sample_line_labels]
    dispersion_multiplier = math.sqrt(widen_dispersion / (ENSEMBLE_SIZE - 1))
    spread = dispersion_multiplier * (sampled - lax.optimization_barrier(jnp.mean(sampled, axis=0, keepdims=True)))
    gram = jnp.dot(spread, spread.T, precision=lax.Precision.HIGHEST, preferred_element_type=jnp.float32)
    cross = jnp.dot(innovation, spread.T, precision=lax.Precision.HIGHEST, preferred_element_type=jnp.float32)
    upper = 1.0 + jnp.sqrt(jnp.sum(gram * gram))
    theta = (upper + 1.0) / 2.0
    delta = (upper - 1.0) / 2.0
    sigma = theta / delta
    rho = 1.0 / sigma
    residual = cross
    direction = residual / theta
    linear_solution = direction
    for turn in range(CHEB - 1):
        residual = residual - direction - jnp.dot(direction, gram, precision=lax.Precision.HIGHEST, preferred_element_type=jnp.float32)
        rho_next = 1.0 / (2.0 * sigma - rho)
        direction = rho_next * rho * direction + 2.0 * rho_next / delta * residual
        linear_solution = linear_solution + direction
        rho = rho_next
    ensemble_combination = math.sqrt(widen_dispersion) * jnp.eye(ENSEMBLE_SIZE, dtype=jnp.float32) + dispersion_multiplier * linear_solution
    flat = propagated_fields.reshape(ENSEMBLE_SIZE, 3 * LATTICE_LINES * POINTS_ACROSS)
    center = lax.optimization_barrier(jnp.mean(flat, axis=0, keepdims=True))
    result = center + jnp.dot(ensemble_combination, flat - center, precision=lax.Precision.HIGHEST, preferred_element_type=jnp.float32)
    return result.reshape(ENSEMBLE_SIZE, 3, LATTICE_LINES, POINTS_ACROSS)
```

```python
import functools
import math

import jax
import jax.numpy as jnp
from jax import lax
from jax.experimental import pallas as pl
from jax.experimental.pallas import tpu as pltpu
from jax.sharding import PartitionSpec as P

STEPS = 4
CHEB = 8
CHUNKS = 4
TILE = 8
EARLY = 2

gravity = 1.0
courant = 0.35
widen_dispersion = 1.1

MESH = pl.DeviceIdType.MESH


def advance(fields):
    depth, east, north = fields
    half = 0.5 * courant
    inverse = 1.0 / depth
    press = 0.5 * gravity * depth * depth
    speed_x = east * inverse
    speed_y = north * inverse
    mixed = east * speed_y
    flux_x = (east, east * speed_x + press, mixed)
    flux_y = (north, mixed, north * speed_y + press)
    rows = depth.shape[0]
    out = []
    for q, fx, fy in zip(fields, flux_x, flux_y):
        quarter = 0.25 * q
        mid = quarter[1:-1]
        kx = half * fx[1:-1]
        sides = pltpu.roll(mid - kx, q.shape[2] - 1, 2) + pltpu.roll(mid + kx, 1, 2)
        up = (quarter - half * fy)[2:]
        down = (quarter + half * fy)[: rows - 2]
        out.append(sides + up + down)
    return tuple(out)


def halves(value):
    high = value.astype(jnp.bfloat16)
    return high, (value - high.astype(jnp.float32)).astype(jnp.bfloat16)


def dot(left, right, dims=((1,), (0,))):
    return lax.dot_general(left, right, (dims, ((), ())), preferred_element_type=jnp.float32)


def dot3(left, right, dims=((1,), (0,))):
    (lh, ll), (rh, rl) = left, right
    return dot(lh, rh, dims) + (dot(lh, rl, dims) + dot(ll, rh, dims))


def kernel(
    dims,
    x_hbm, loc_ref, depth_ref, inv_ref, draw_hbm, label_ref,
    out_hbm,
    prior, draw, halo, stepped, everyone, result, sampled, noise,
    st_hi, st_lo, basis, gain_hi, gain_lo,
    load_sem, draw_sem, halo_send, halo_recv, s_send, s_recv, n_send, n_recv,
    f_send, f_recv, b_send, b_recv, own_sem,
):
    nz, nx, nc, ny = dims
    z = lax.axis_index("role")
    grp = lax.axis_index("grp")
    y = lax.axis_index("run")
    x = grp // nc
    c = grp % nc
    rows, _, members, cols = prior.shape
    obs = loc_ref.shape[1]
    total = nz * nx * nc * members
    width = STEPS

    def device(zz, xx, cc, yy):
        return (zz, xx * nc + cc, yy)

    def flat(cc, xx, zz):
        return (cc * nx + xx) * nz + zz

    def row_of(cc, xx, zz):
        return lax.rem((nc - 1 - cc) * nx * nz + width + xx * nz + zz, rows)

    me = flat(c, x, z)
    my_row = row_of(c, x, z)
    other_x = lax.rem(x + 1, nx)
    other_y = lax.rem(y + 1, ny)
    other_c = lax.rem(c + 1, nc)
    z_far = lax.rem(z + 2, nz)
    z_near = z + 1 - 2 * lax.rem(z, 2)
    z_cross = lax.rem(z_near + 2, nz)

    offsets = [(2, 1), (2, 0), (1, 1), (1, 0), (3, 1), (3, 0), (0, 1)]

    barrier = pltpu.get_barrier_semaphore()
    for dz, dx in offsets:
        for cc in range(nc):
            pl.semaphore_signal(
                barrier, inc=1, device_id=device(lax.rem(z + dz, nz), lax.rem(x + dx, nx), cc, y), device_id_type=MESH
            )
    pl.semaphore_signal(barrier, inc=1, device_id=device(z, x, other_c, y), device_id_type=MESH)
    pl.semaphore_signal(barrier, inc=1, device_id=device(z, x, c, other_y), device_id_type=MESH)

    loads = []
    for r in range(rows):
        for f in range(3):
            copy = pltpu.make_async_copy(x_hbm.at[:, f, r], prior.at[r, f], load_sem.at[r, f])
            copy.start()
            loads.append(copy)
    draw_copy = pltpu.make_async_copy(draw_hbm, draw, draw_sem)
    draw_copy.start()
    for copy in loads:
        copy.wait()

    def inner(t, carry):
        at = pl.ds(pl.multiple_of(t * TILE, TILE), TILE)
        fields = tuple(prior[:, f, at] for f in range(3))
        for step in range(STEPS):
            fields = advance(fields)
        for f in range(3):
            stepped[width : rows - width, f, at] = fields[f]
        return carry

    lax.fori_loop(0, members // TILE, inner, 0)

    pl.semaphore_wait(barrier, 2 * len(offsets) + 2)

    def remote(src, dst, send, recv, target):
        return pltpu.make_async_remote_copy(
            src_ref=src, dst_ref=dst, send_sem=send, recv_sem=recv, device_id=target, device_id_type=MESH
        )

    per = members // CHUNKS
    halo_copies = []
    for k in range(CHUNKS):
        part = pl.ds(k * per, per)
        pair = (
            remote(prior.at[pl.ds(rows - width, width), :, part], halo.at[0, :, :, part],
                   halo_send.at[2 * k], halo_recv.at[2 * k], device(z, x, c, other_y)),
            remote(prior.at[pl.ds(0, width), :, part], halo.at[1, :, :, part],
                   halo_send.at[2 * k + 1], halo_recv.at[2 * k + 1], device(z, x, c, other_y)),
        )
        for copy in pair:
            copy.start()
        halo_copies.append(pair)

    def sender(cc, dz, dx):
        zz, xx = lax.rem(z + dz, nz), lax.rem(x + dx, nx)
        k = dz * nx + dx
        return remote(stepped.at[row_of(cc, xx, zz)], everyone.at[me], f_send.at[cc, k], f_recv.at[c, k],
                      device(zz, xx, cc, y))

    inner_sends = [sender(1, dz, dx) for dz, dx in offsets]
    edge_sends = [sender(0, dz, dx) for dz, dx in offsets]
    core_send = remote(stepped.at[row_of(other_c, x, z)], everyone.at[me], f_send.at[other_c, 0], f_recv.at[c, 0],
                       device(z, x, other_c, y))
    for copy in inner_sends[:EARLY]:
        copy.start()

    def gather(buf, send, recv):
        def hop(i, src, target):
            return remote(src, src, send.at[i], recv.at[i], target)

        return {
            "far": hop(0, buf.at[c, y, x, z], device(z_far, x, c, y)),
            "near": hop(1, buf.at[c, y, x, z], device(z_near, x, c, y)),
            "relay": hop(2, buf.at[c, y, x, z_far], device(z_near, x, c, y)),
            "x": hop(3, buf.at[c, y, x], device(z, other_x, c, y)),
            "y0": hop(4, buf.at[c, y, x, z], device(z, x, c, other_y)),
            "y1": hop(5, buf.at[c, y, x, z_far], device(z, x, c, other_y)),
            "y2": hop(6, buf.at[c, y, x, z_near], device(z, x, c, other_y)),
            "y3": hop(7, buf.at[c, y, x, z_cross], device(z, x, c, other_y)),
            "y4": hop(8, buf.at[c, y, other_x], device(z, x, c, other_y)),
            "c0": hop(9, buf.at[c, y], device(z, x, other_c, y)),
            "c1": hop(10, buf.at[c, other_y], device(z, x, other_c, y)),
        }

    s = gather(sampled, s_send, s_recv)
    n = gather(noise, n_send, n_recv)

    loc = loc_ref[...]
    scale = inv_ref[...]
    lanes = lax.broadcasted_iota(jnp.int32, (2 * cols, obs), 0)

    def pick(r, acc):
        hot = jnp.where(loc - r * cols == lanes, 1.0, 0.0).astype(jnp.bfloat16)
        depth = jnp.concatenate([stepped[r, 0], stepped[r + 1, 0]], 1)
        d1 = depth.astype(jnp.bfloat16)
        rest = depth - d1.astype(jnp.float32)
        d2 = rest.astype(jnp.bfloat16)
        d3 = (rest - d2.astype(jnp.float32)).astype(jnp.bfloat16)
        return acc + (dot(d1, hot) + (dot(d2, hot) + dot(d3, hot)))

    picked = jnp.zeros((members, obs), jnp.float32)
    for r in range(width, rows - width, 2):
        picked = pick(r, picked)

    draw_copy.wait()
    base = scale * depth_ref[...]

    def line(i, carry):
        noise[c, y, x, z, pl.ds(i, 1)] = base + draw[pl.ds(label_ref[i], 1)]
        return carry

    lax.fori_loop(0, members, line, 0)
    n["far"].start()
    n["near"].start()

    for k in range(CHUNKS):
        for copy in halo_copies[k]:
            copy.wait_recv()

        def edge(t, carry):
            at = pl.ds(pl.multiple_of(k * per + t * TILE, TILE), TILE)
            for side in range(2):
                low, high = (0, 2 * width) if side == 0 else (rows - 2 * width, rows)
                fields = []
                for f in range(3):
                    own = prior[low:high, f, at]
                    fields.append(jnp.concatenate([halo[0, :, f, at], own] if side == 0 else [own, halo[1, :, f, at]], 0))
                for step in range(STEPS):
                    fields = advance(fields)
                first = 0 if side == 0 else rows - width
                for f in range(3):
                    stepped[first : first + width, f, at] = fields[f]
            return carry

        lax.fori_loop(0, per // TILE, edge, 0)

    for r in list(range(0, width, 2)) + list(range(rows - width, rows, 2)):
        picked = pick(r, picked)
    sampled[c, y, x, z] = scale * picked
    s["far"].start()
    s["near"].start()
    s["y0"].start()

    core_send.start()
    for copy in inner_sends[EARLY:]:
        copy.start()
    for copy in edge_sends:
        copy.start()
    everyone[me] = stepped[my_row]
    n["far"].wait_recv()
    n["relay"].start()

    s["far"].wait_recv()
    s["relay"].start()
    s["y1"].start()
    s["near"].wait_recv()
    s["y2"].start()
    s["relay"].wait_recv()
    s["x"].start()
    s["y3"].start()
    n["near"].wait_recv()
    n["relay"].wait_recv()
    n["x"].start()
    s["x"].wait_recv()
    s["y4"].start()
    s["c0"].start()
    n["x"].wait_recv()
    for i in range(5):
        n["y" + str(i)].start()
    n["c0"].start()

    dispersion = math.sqrt(widen_dispersion / (total - 1))

    def spread(yy):
        block = sampled[:, yy].reshape(total, obs)
        value = dispersion * (block - jnp.sum(block, axis=0, keepdims=True) * (1.0 / total))
        hi, lo = halves(value.T)
        at = pl.ds(pl.multiple_of(yy * obs, obs), obs)
        st_hi[at] = hi
        st_lo[at] = lo

    s["c0"].wait_recv()
    spread(y)
    for i in range(5):
        s["y" + str(i)].wait_recv()
    s["c1"].start()
    s["c1"].wait_recv()
    spread(other_y)

    nt = ((1,), (1,))
    every = ny * obs
    sth = st_hi[...]
    stl = st_lo[...]
    gram = dot3((sth, stl), (sth, stl), nt)
    upper = 1.0 + jnp.sqrt(jnp.sum(jnp.sum(gram * gram, axis=1, keepdims=True), axis=0, keepdims=True))
    theta = (upper + 1.0) / 2.0
    delta = (upper - 1.0) / 2.0
    sigma = theta / delta
    rho = [1.0 / sigma]
    lead = [1.0 / theta]
    fade = rho[0]
    for turn in range(1, CHEB):
        rho.append(1.0 / (2.0 * sigma - rho[-1]))
        lead.append(2.0 * rho[-1] / delta * fade)
        fade = fade * rho[-1]
    weight = [None] * CHEB
    tail = jnp.ones_like(theta)
    for turn in reversed(range(CHEB)):
        weight[turn] = lead[turn] * tail
        tail = 1.0 + rho[turn] * rho[turn - 1] * tail
    eye = jnp.where(
        lax.broadcasted_iota(jnp.int32, (every, every), 0) == lax.broadcasted_iota(jnp.int32, (every, every), 1),
        1.0, 0.0,
    )
    t1 = eye - gram / delta
    basis[0] = t1
    h1 = halves(t1)
    t2 = 2.0 * dot3(h1, h1) - eye
    basis[1] = t2
    h2 = halves(t2)
    t3 = 2.0 * dot3(h1, h2) - basis[0]
    basis[2] = t3
    t4 = 2.0 * dot3(h2, h2) - eye
    upper_part = weight[5] * basis[0] + weight[6] * basis[1] + weight[7] * basis[2]
    lower_part = (
        weight[0] * eye
        + (weight[1] - weight[7]) * basis[0]
        + (weight[2] - weight[6]) * basis[1]
        + (weight[3] - weight[5]) * basis[2]
        + weight[4] * t4
    )
    basis[3] = dispersion * (lower_part + 2.0 * dot3(halves(t4), halves(upper_part)))

    for i in range(5):
        n["y" + str(i)].wait_recv()
    n["c0"].wait_recv()
    n["c1"].start()
    n["c1"].wait_recv()

    for cc in range(nc):
        part = jnp.concatenate(
            [noise[cc, yy].reshape(total // nc, obs) - sampled[cc, yy].reshape(total // nc, obs) for yy in range(ny)], 1
        )
        hi, lo = halves(dot3(halves(part), halves(basis[3])))
        gain_hi[pl.ds(cc * (total // nc), total // nc)] = hi
        gain_lo[pl.ds(cc * (total // nc), total // nc)] = lo

    for dz, dx in offsets:
        for cc in range(nc):
            k = dz * nx + dx
            zz, xx = lax.rem(z + nz - dz, nz), lax.rem(x + dx, nx)
            at = flat(cc, xx, zz)
            remote(stepped.at[0], everyone.at[at], f_send.at[0, k], f_recv.at[cc, k], device(zz, xx, cc, y)).wait_recv()
    at = flat(other_c, x, z)
    remote(stepped.at[0], everyone.at[at], f_send.at[0, 0], f_recv.at[other_c, 0], device(z, x, other_c, y)).wait_recv()

    center = []
    devs = []
    for f in range(3):
        values = everyone[:, f].reshape(total, cols)
        mean = jnp.sum(values, axis=0, keepdims=True) * (1.0 / total)
        center.append(mean)
        devs.append(values - mean)
    cross = dot3((st_hi[...], st_lo[...]), halves(jnp.concatenate(devs, 1)))
    chi, clo = halves(cross)

    def analyse(cc, xx, zz):
        at = flat(cc, xx, zz)
        own = pl.ds(pl.multiple_of(at * members, members), members)
        gain = dot3((gain_hi[own], gain_lo[own]), (chi, clo))
        for f in range(3):
            result[at, f] = (
                center[f]
                + math.sqrt(widen_dispersion) * (everyone[at, f] - center[f])
                + gain[:, f * cols : (f + 1) * cols]
            )
        return at

    for dz, dx in offsets:
        for cc in range(nc):
            zz, xx = lax.rem(z + dz, nz), lax.rem(x + dx, nx)
            k = dz * nx + dx
            at = analyse(cc, xx, zz)
            for f in range(3):
                remote(result.at[at, f], out_hbm.at[:, f, my_row], b_send.at[cc, k, f], b_recv.at[c, k, f],
                       device(zz, xx, cc, y)).start()
    at = analyse(other_c, x, z)
    for f in range(3):
        remote(result.at[at, f], out_hbm.at[:, f, my_row], b_send.at[other_c, 0, f], b_recv.at[c, 0, f],
               device(z, x, other_c, y)).start()
    at = analyse(c, x, z)
    own_copies = []
    for f in range(3):
        copy = pltpu.make_async_copy(result.at[at, f], out_hbm.at[:, f, my_row], own_sem.at[f])
        copy.start()
        own_copies.append(copy)

    for copy in halo_copies:
        for half in copy:
            half.wait_send()
    for copy in list(s.values()) + list(n.values()) + inner_sends + edge_sends + [core_send]:
        copy.wait_send()
    for dz, dx in offsets:
        for cc in range(nc):
            k = dz * nx + dx
            zz, xx = lax.rem(z + nz - dz, nz), lax.rem(x + dx, nx)
            row = row_of(cc, xx, zz)
            for f in range(3):
                copy = remote(result.at[0, f], out_hbm.at[:, f, row], b_send.at[cc, k, f], b_recv.at[cc, k, f],
                              device(zz, xx, cc, y))
                copy.wait_send()
                copy.wait_recv()
    for f in range(3):
        copy = remote(result.at[0, f], out_hbm.at[:, f, row_of(other_c, x, z)], b_send.at[other_c, 0, f],
                      b_recv.at[other_c, 0, f], device(z, x, other_c, y))
        copy.wait_send()
        copy.wait_recv()
    for copy in own_copies:
        copy.wait()


def with_halo(cells, sides, width):
    for axis, dim in sides:
        count = lax.axis_size(axis)
        head = lax.slice_in_dim(cells, 0, width, axis=dim)
        tail = lax.slice_in_dim(cells, cells.shape[dim] - width, cells.shape[dim], axis=dim)
        cells = jnp.concatenate(
            [
                lax.ppermute(tail, axis, [(i, (i + 1) % count) for i in range(count)]),
                cells,
                lax.ppermute(head, axis, [((i + 1) % count, i) for i in range(count)]),
            ],
            axis=dim,
        )
    return cells


def lax_friedrichs(state):
    depth = state[:, 0]
    east = state[:, 1]
    north = state[:, 2]
    press = 0.5 * gravity * depth * depth
    flux_x = jnp.stack([east, east * east / depth + press, east * north / depth], 1)
    flux_y = jnp.stack([north, east * north / depth, north * north / depth + press], 1)
    inner = state[:, :, 1:-1]
    average = 0.25 * (
        state[:, :, 2:] + state[:, :, :-2] + jnp.roll(inner, 1, 3) + jnp.roll(inner, -1, 3)
    )
    middle = flux_x[:, :, 1:-1]
    return (
        average
        - 0.5 * courant * (jnp.roll(middle, -1, 3) - jnp.roll(middle, 1, 3))
        - 0.5 * courant * (flux_y[:, :, 2:] - flux_y[:, :, :-2])
    )


def product(left, right):
    return jnp.dot(left, right, precision=lax.Precision.HIGHEST, preferred_element_type=jnp.float32)


def plain(
    prior_fields,
    measured_point_location,
    measured_depths,
    inverse_noise_deviation,
    sample_noise_draw,
    sample_line_labels,
):
    dispersion_multiplier = math.sqrt(widen_dispersion / (sample_noise_draw.shape[0] - 1))
    propagated_fields = prior_fields
    for step in range(STEPS):
        padded = with_halo(propagated_fields, (("run", 2),), 1)
        propagated_fields = lax_friedrichs(padded)
    members = propagated_fields.shape[0]
    depth_flat = propagated_fields[:, 0].reshape(
        members, propagated_fields.shape[2] * propagated_fields.shape[3]
    )
    sampled = inverse_noise_deviation[None, :] * jnp.take(
        depth_flat, measured_point_location, axis=1
    )
    innovation = (
        inverse_noise_deviation[None, :] * measured_depths[None, :]
        - sampled
        + jnp.take(sample_noise_draw, sample_line_labels, axis=0)
    )
    all_sampled, all_innov = (
        lax.all_gather(sampled, ("role", "grp"), axis=0, tiled=True),
        lax.all_gather(innovation, ("role", "grp"), axis=0, tiled=True),
    )
    spread = dispersion_multiplier * (all_sampled - jnp.mean(all_sampled, axis=0, keepdims=True))
    first = lax.axis_index(("role", "grp")) * members
    own_spread = lax.dynamic_slice_in_dim(spread, first, members, 0)
    own_innov = lax.dynamic_slice_in_dim(all_innov, first, members, 0)
    gram_rows, cross_rows = (
        lax.psum_scatter(product(own_spread, spread.T), "run", scatter_dimension=0, tiled=True),
        lax.psum_scatter(product(own_innov, spread.T), "run", scatter_dimension=0, tiled=True),
    )
    gram = lax.all_gather(gram_rows, ("role", "grp", "run"), axis=0, tiled=True)
    upper = 1.0 + jnp.sqrt(jnp.sum(gram * gram))
    theta = (upper + 1.0) / 2.0
    delta = (upper - 1.0) / 2.0
    sigma = theta / delta
    rho = 1.0 / sigma
    residual = cross_rows
    direction = residual / theta
    linear_solution = direction
    for turn in range(CHEB - 1):
        residual = residual - direction - product(direction, gram)
        rho_next = 1.0 / (2.0 * sigma - rho)
        direction = rho_next * rho * direction + 2.0 * rho_next / delta * residual
        linear_solution = linear_solution + direction
        rho = rho_next
    posterior_coefficients = lax.all_gather(
        linear_solution, ("role", "grp", "run"), axis=0, tiled=True
    )
    ensemble_combination = (
        math.sqrt(widen_dispersion) * jnp.eye(posterior_coefficients.shape[0], dtype=jnp.float32)
        + dispersion_multiplier * posterior_coefficients
    )
    strip_slab = lax.all_to_all(
        propagated_fields, ("role", "grp"), split_axis=2, concat_axis=0, tiled=True
    )
    array_shape = strip_slab.shape
    flat = strip_slab.reshape(array_shape[0], array_shape[1] * array_shape[2] * array_shape[3])
    center = jnp.mean(flat, axis=0, keepdims=True)
    updated = (center + product(ensemble_combination, flat - center)).reshape(array_shape)
    return lax.all_to_all(updated, ("role", "grp"), split_axis=0, concat_axis=2, tiled=True)


def fused(
    dims,
    prior_fields,
    measured_point_location,
    measured_depths,
    inverse_noise_deviation,
    sample_noise_draw,
    sample_line_labels,
):
    nz, nx, nc, ny = dims
    members, _, rows, cols = prior_fields.shape
    obs = measured_point_location.shape[0]
    every = ny * obs
    group = nz * nx * nc
    slab = (group, 3, members, cols)
    gathered = (nc, ny, nx, nz, members, obs)
    total = group * members
    dma = pltpu.SemaphoreType.DMA
    vmem = pl.BlockSpec(memory_space=pltpu.VMEM)
    anywhere = pl.BlockSpec(memory_space=pl.ANY)
    hops = 11
    return pl.pallas_call(
        functools.partial(kernel, dims),
        out_shape=jax.ShapeDtypeStruct(prior_fields.shape, jnp.float32),
        in_specs=[anywhere, vmem, vmem, vmem, anywhere, pl.BlockSpec(memory_space=pltpu.SMEM)],
        out_specs=anywhere,
        scratch_shapes=[
            pltpu.VMEM((rows, 3, members, cols), jnp.float32),
            pltpu.VMEM(sample_noise_draw.shape, jnp.float32),
            pltpu.VMEM((2, STEPS, 3, members, cols), jnp.float32),
            pltpu.VMEM((rows, 3, members, cols), jnp.float32),
            pltpu.VMEM(slab, jnp.float32),
            pltpu.VMEM(slab, jnp.float32),
            pltpu.VMEM(gathered, jnp.float32),
            pltpu.VMEM(gathered, jnp.float32),
            pltpu.VMEM((every, total), jnp.bfloat16),
            pltpu.VMEM((every, total), jnp.bfloat16),
            pltpu.VMEM((4, every, every), jnp.float32),
            pltpu.VMEM((total, every), jnp.bfloat16),
            pltpu.VMEM((total, every), jnp.bfloat16),
            dma((rows, 3)),
            dma,
            dma((2 * CHUNKS,)),
            dma((2 * CHUNKS,)),
            dma((hops,)),
            dma((hops,)),
            dma((hops,)),
            dma((hops,)),
            dma((nc, nz * nx)),
            dma((nc, nz * nx)),
            dma((nc, nz * nx, 3)),
            dma((nc, nz * nx, 3)),
            dma((3,)),
        ],
        compiler_params=pltpu.CompilerParams(
            collective_id=0, has_side_effects=True, vmem_limit_bytes=60 * 1024 * 1024
        ),
        name="analysis_kernel",
    )(
        prior_fields,
        measured_point_location[None, :],
        measured_depths[None, :],
        inverse_noise_deviation[None, :],
        sample_noise_draw,
        sample_line_labels,
    )


def shards(shape, *args):
    nz, grp, ny = shape["role"], shape["grp"], shape["run"]
    members, _, rows, cols = args[0].shape
    fits = (
        grp == 4
        and ny == 2
        and nz == 4
        and rows == nz * grp
        and rows == 4 * STEPS
        and CHEB == 8
        and members % (CHUNKS * TILE) == 0
        and cols == 128
        and args[1].shape[0] * ny <= 512
    )
    if fits:
        return fused((nz, 2, 2, ny), *args)
    return plain(*args)


def solution(mesh):
    placed = (
        P(("role", "grp"), None, "run", None),
        P("run"),
        P("run"),
        P("run"),
        P(None, "run"),
        P(("role", "grp")),
    )
    return jax.shard_map(
        functools.partial(shards, dict(mesh.shape)),
        mesh=mesh,
        in_specs=placed,
        out_specs=P(("role", "grp"), None, "run", None),
        check_vma=False,
    )
```

```python
import functools
import math

import jax
import jax.numpy as jnp
from jax import lax
from jax.experimental import pallas as pl
from jax.experimental.pallas import tpu as pltpu
from jax.sharding import PartitionSpec as P

STEPS = 4
CHEB = 8
CHUNKS = 4
TILE = 8
FIRST = (0, 1, 2, 6)
SECOND = (3,)
THIRD = (7,)
FOURTH = (8,)

gravity = 1.0
courant = 0.35
widen_dispersion = 1.1

MESH = pl.DeviceIdType.MESH


def advance(fields):
    depth, east, north = fields
    half = 0.5 * courant
    inverse = 1.0 / depth
    press = 0.5 * gravity * depth * depth
    speed_x = east * inverse
    speed_y = north * inverse
    mixed = east * speed_y
    flux_x = (east, east * speed_x + press, mixed)
    flux_y = (north, mixed, north * speed_y + press)
    rows = depth.shape[0]
    out = []
    for q, fx, fy in zip(fields, flux_x, flux_y):
        quarter = 0.25 * q
        mid = quarter[1:-1]
        kx = half * fx[1:-1]
        sides = pltpu.roll(mid - kx, q.shape[2] - 1, 2) + pltpu.roll(mid + kx, 1, 2)
        up = (quarter - half * fy)[2:]
        down = (quarter + half * fy)[: rows - 2]
        out.append(sides + up + down)
    return tuple(out)


def halves(value):
    high = value.astype(jnp.bfloat16)
    return high, (value - high.astype(jnp.float32)).astype(jnp.bfloat16)


def dot(left, right, dims=((1,), (0,))):
    return lax.dot_general(left, right, (dims, ((), ())), preferred_element_type=jnp.float32)


def dot3(left, right, dims=((1,), (0,))):
    (lh, ll), (rh, rl) = left, right
    return dot(lh, rh, dims) + (dot(lh, rl, dims) + dot(ll, rh, dims))


def kernel(
    dims,
    x_hbm, loc_ref, depth_ref, inv_ref, draw_hbm, label_ref,
    out_hbm,
    prior, draw, halo, stepped, everyone, result, sampled, noise,
    st_hi, st_lo, basis,
    load_sem, draw_sem, halo_send, halo_recv, s_send, s_recv, n_send, n_recv,
    f_send, f_recv, b_send, b_recv, own_sem, plane, full,
):
    nz, nx, nc, ny = dims
    z = lax.axis_index("role")
    grp = lax.axis_index("grp")
    y = lax.axis_index("run")
    x = grp // nc
    c = grp % nc
    rows, _, members, cols = prior.shape
    obs = loc_ref.shape[1]
    total = nz * nx * nc * members
    width = STEPS

    def device(zz, xx, cc, yy):
        return (zz, xx * nc + cc, yy)

    def flat(cc, xx, zz):
        return (cc * nx + xx) * nz + zz

    def row_of(cc, xx, zz):
        return lax.rem((nc - 1 - cc) * nx * nz + width + xx * nz + zz, rows)

    me = flat(c, x, z)
    my_row = row_of(c, x, z)
    other_x = lax.rem(x + 1, nx)
    other_y = lax.rem(y + 1, ny)
    other_c = lax.rem(c + 1, nc)
    z_far = lax.rem(z + 2, nz)
    z_near = z + 1 - 2 * lax.rem(z, 2)
    z_cross = lax.rem(z_near + 2, nz)

    zs = [z, z_near, z_far, z_cross]
    offsets = [(2, 0), (3, 0), (2, 1), (3, 1), (1, 0), (1, 1), (0, 1)]

    def partner(q, dx):
        return zs[q], lax.rem(x + dx, nx)

    barrier = pltpu.get_barrier_semaphore()
    targets = [device(*partner(q, dx), 1, y) for q, dx in offsets]
    targets += [device(z, x, other_c, y), device(z, x, 0, other_y)]
    for target in targets:
        pl.semaphore_signal(barrier, inc=1, device_id=target, device_id_type=MESH)

    loads = []
    for r in range(rows):
        for f in range(3):
            copy = pltpu.make_async_copy(x_hbm.at[:, f, r], prior.at[r, f], load_sem.at[r, f])
            copy.start()
            loads.append(copy)
    draw_copy = pltpu.make_async_copy(draw_hbm, draw, draw_sem)
    draw_copy.start()
    for copy in loads:
        copy.wait()

    @pl.when(c == 0)
    def _():
        pl.semaphore_wait(barrier, 3)
        pl.semaphore_signal(plane, inc=1, device_id=device(z, x, 1, y), device_id_type=MESH)

    @pl.when(c == 1)
    def _():
        pl.semaphore_wait(plane, 1)

    def remote(src, dst, send, recv, target):
        return pltpu.make_async_remote_copy(
            src_ref=src, dst_ref=dst, send_sem=send, recv_sem=recv, device_id=target, device_id_type=MESH
        )

    per = members // CHUNKS
    halo_copies = []
    for k in range(CHUNKS):
        part = pl.ds(k * per, per)
        pair = (
            remote(prior.at[pl.ds(rows - width, width), :, part], halo.at[0, :, :, part],
                   halo_send.at[2 * k], halo_recv.at[2 * k], device(z, x, c, other_y)),
            remote(prior.at[pl.ds(0, width), :, part], halo.at[1, :, :, part],
                   halo_send.at[2 * k + 1], halo_recv.at[2 * k + 1], device(z, x, c, other_y)),
        )
        for copy in pair:
            copy.start()
        halo_copies.append(pair)

    scale = inv_ref[...]
    base = scale * depth_ref[...]
    draw_copy.wait()

    def line(i, carry):
        for j in range(TILE):
            at = i * TILE + j
            noise[c, y, x, z, pl.ds(at, 1)] = base + draw[pl.ds(label_ref[at], 1)]
        return carry

    lax.fori_loop(0, members // TILE, line, 0)

    def inner(t, carry):
        at = pl.ds(pl.multiple_of(t * TILE, TILE), TILE)
        fields = tuple(prior[:, f, at] for f in range(3))
        for step in range(STEPS):
            fields = advance(fields)
        for f in range(3):
            stepped[width : rows - width, f, at] = fields[f]
        return carry

    lax.fori_loop(0, members // TILE, inner, 0)

    @pl.when(c == 1)
    def _():
        pl.semaphore_wait(barrier, nc * len(offsets) + 1)
        pl.semaphore_signal(full, inc=1, device_id=device(z, x, 0, y), device_id_type=MESH)

    @pl.when(c == 0)
    def _():
        pl.semaphore_wait(full, 1)

    def sender(cc, q, dx):
        zz, xx = partner(q, dx)
        k = q * nx + dx
        return remote(stepped.at[row_of(cc, xx, zz)], everyone.at[me], f_send.at[cc, k], f_recv.at[c, k],
                      device(zz, xx, cc, y))

    inner_sends = [sender(1, q, dx) for q, dx in offsets]
    edge_sends = [sender(0, q, dx) for q, dx in offsets]
    core_send = remote(stepped.at[row_of(other_c, x, z)], everyone.at[me], f_send.at[other_c, 0], f_recv.at[c, 0],
                       device(z, x, other_c, y))
    def gather(buf, send, recv):
        def hop(i, src, target):
            return remote(src, src, send.at[i], recv.at[i], target)

        out = {
            "far": hop(0, buf.at[c, y, x, z], device(z_far, x, c, y)),
            "near": hop(1, buf.at[c, y, x, z], device(z_near, x, c, y)),
            "relay": hop(2, buf.at[c, y, x, z_far], device(z_near, x, c, y)),
            "c0": hop(15, buf.at[c, y, x], device(z, x, other_c, y)),
            "c1": hop(16, buf.at[c, y, other_x], device(z, x, other_c, y)),
            "c2": hop(17, buf.at[c, other_y, x], device(z, x, other_c, y)),
            "c3": hop(18, buf.at[c, other_y, other_x], device(z, x, other_c, y)),
        }
        for q in range(nz):
            block = buf.at[c, y, x, zs[q]]
            out["x", q] = hop(3 + q, block, device(z, other_x, c, y))
            out["y", q] = hop(7 + q, block, device(z, x, c, other_y))
            out["w", q] = hop(11 + q, buf.at[c, y, other_x, zs[q]], device(z, x, c, other_y))
        return out

    def start(g, *names):
        for name in names:
            g[name].start()

    def arrive(g, *names):
        for name in names:
            g[name].wait_recv()

    s = gather(sampled, s_send, s_recv)
    n = gather(noise, n_send, n_recv)
    start(n, "far", "near", ("x", 0))
    for i in FIRST:
        inner_sends[i].start()

    loc = loc_ref[...]
    lanes = lax.broadcasted_iota(jnp.int32, (2 * cols, obs), 0)

    def pick(r, acc):
        hot = jnp.where(loc - r * cols == lanes, 1.0, 0.0).astype(jnp.bfloat16)
        depth = jnp.concatenate([stepped[r, 0], stepped[r + 1, 0]], 1)
        d1 = depth.astype(jnp.bfloat16)
        rest = depth - d1.astype(jnp.float32)
        d2 = rest.astype(jnp.bfloat16)
        d3 = (rest - d2.astype(jnp.float32)).astype(jnp.bfloat16)
        return acc + (dot(d1, hot) + (dot(d2, hot) + dot(d3, hot)))

    picked = jnp.zeros((members, obs), jnp.float32)
    for r in range(width, rows - width, 2):
        picked = pick(r, picked)

    arrive(n, "far")
    start(n, "relay", ("x", 2))

    for k in range(CHUNKS):
        for copy in halo_copies[k]:
            copy.wait_recv()

        def edge(t, carry):
            at = pl.ds(pl.multiple_of(k * per + t * TILE, TILE), TILE)
            for side in range(2):
                low, high = (0, 2 * width) if side == 0 else (rows - 2 * width, rows)
                fields = []
                for f in range(3):
                    own = prior[low:high, f, at]
                    fields.append(jnp.concatenate([halo[0, :, f, at], own] if side == 0 else [own, halo[1, :, f, at]], 0))
                for step in range(STEPS):
                    fields = advance(fields)
                first = 0 if side == 0 else rows - width
                for f in range(3):
                    stepped[first : first + width, f, at] = fields[f]
            return carry

        lax.fori_loop(0, per // TILE, edge, 0)
        if k == 1:
            arrive(n, "near", "relay")
            start(n, ("x", 1), ("x", 3))

    for r in list(range(0, width, 2)) + list(range(rows - width, rows, 2)):
        picked = pick(r, picked)
    sampled[c, y, x, z] = scale * picked
    start(s, "far", "near", ("x", 0), ("y", 0))
    for i in SECOND:
        (inner_sends + edge_sends)[i].start()
    core_send.start()
    everyone[me] = stepped[my_row]
    arrive(s, "far")
    start(s, "relay", ("x", 2), ("y", 2))
    for i in THIRD:
        (inner_sends + edge_sends)[i].start()
    arrive(s, "near")
    start(s, ("x", 1), ("y", 1))
    arrive(s, "relay")
    start(s, ("x", 3), ("y", 3), "c0")
    for i in FOURTH:
        (inner_sends + edge_sends)[i].start()
    for q in (0, 2, 1, 3):
        arrive(s, ("x", q))
        start(s, ("w", q))
    start(s, "c1")
    for i, copy in enumerate(inner_sends + edge_sends):
        if i not in FIRST + SECOND + THIRD + FOURTH:
            copy.start()
    start(n, *[("y", q) for q in range(nz)])
    start(n, "c0")
    arrive(n, *[("x", q) for q in range(nz)])
    start(n, *[("w", q) for q in range(nz)])
    start(n, "c1")

    dispersion = math.sqrt(widen_dispersion / (total - 1))

    def spread(yy):
        block = sampled[:, yy].reshape(total, obs)
        value = dispersion * (block - jnp.sum(block, axis=0, keepdims=True) * (1.0 / total))
        hi, lo = halves(value.T)
        at = pl.ds(pl.multiple_of(yy * obs, obs), obs)
        st_hi[at] = hi
        st_lo[at] = lo

    arrive(s, "c0", "c1")
    spread(y)
    arrive(s, *[("y", q) for q in range(nz)])
    start(s, "c2")
    arrive(s, *[("w", q) for q in range(nz)])
    start(s, "c3")
    arrive(s, "c2", "c3")
    spread(other_y)

    nt = ((1,), (1,))
    every = ny * obs
    sth = st_hi[...]
    stl = st_lo[...]
    gram = dot3((sth, stl), (sth, stl), nt)
    upper = 1.0 + jnp.sqrt(jnp.sum(jnp.sum(gram * gram, axis=1, keepdims=True), axis=0, keepdims=True))
    theta = (upper + 1.0) / 2.0
    delta = (upper - 1.0) / 2.0
    sigma = theta / delta
    rho = [1.0 / sigma]
    lead = [1.0 / theta]
    fade = rho[0]
    for turn in range(1, CHEB):
        rho.append(1.0 / (2.0 * sigma - rho[-1]))
        lead.append(2.0 * rho[-1] / delta * fade)
        fade = fade * rho[-1]
    weight = [None] * CHEB
    tail = jnp.ones_like(theta)
    for turn in reversed(range(CHEB)):
        weight[turn] = lead[turn] * tail
        tail = 1.0 + rho[turn] * rho[turn - 1] * tail
    eye = jnp.where(
        lax.broadcasted_iota(jnp.int32, (every, every), 0) == lax.broadcasted_iota(jnp.int32, (every, every), 1),
        1.0, 0.0,
    )
    t1 = eye - gram * (1.0 / delta)
    basis[0] = t1
    h1 = halves(t1)
    t2 = 2.0 * dot3(h1, h1) - eye
    basis[1] = t2
    h2 = halves(t2)
    t3 = 2.0 * dot3(h1, h2) - basis[0]
    basis[2] = t3
    t4 = 2.0 * dot3(h2, h2) - eye
    upper_part = weight[5] * basis[0] + weight[6] * basis[1] + weight[7] * basis[2]
    lower_part = (
        weight[0] * eye
        + (weight[1] - weight[7]) * basis[0]
        + (weight[2] - weight[6]) * basis[1]
        + (weight[3] - weight[5]) * basis[2]
        + weight[4] * t4
    )
    basis[3] = dispersion * (lower_part + 2.0 * dot3(halves(t4), halves(upper_part)))

    for q, dx in offsets:
        for cc in range(nc):
            k = q * nx + dx
            zz, xx = partner(q, dx)
            remote(stepped.at[0], everyone.at[flat(cc, xx, zz)], f_send.at[0, k], f_recv.at[cc, k],
                   device(zz, xx, cc, y)).wait_recv()
    remote(stepped.at[0], everyone.at[flat(other_c, x, z)], f_send.at[0, 0], f_recv.at[other_c, 0],
           device(z, x, other_c, y)).wait_recv()

    center = []
    devs = []
    for f in range(3):
        values = everyone[:, f].reshape(total, cols)
        mean = jnp.sum(values, axis=0, keepdims=True) * (1.0 / total)
        center.append(mean)
        devs.append(values - mean)
    cross = dot3((st_hi[...], st_lo[...]), halves(jnp.concatenate(devs, 1)))
    whi, wlo = halves(dot3(halves(basis[3]), halves(cross)))

    arrive(n, *[("y", q) for q in range(nz)])
    start(n, "c2")
    arrive(n, *[("w", q) for q in range(nz)])
    start(n, "c3")
    arrive(n, "c0", "c1", "c2", "c3")

    def analyse(cc, xx, zz):
        at = flat(cc, xx, zz)
        innov = jnp.concatenate([noise[cc, yy, xx, zz] - sampled[cc, yy, xx, zz] for yy in range(ny)], 1)
        gain = dot3(halves(innov), (whi, wlo))
        for f in range(3):
            result[at, f] = (
                center[f]
                + math.sqrt(widen_dispersion) * (everyone[at, f] - center[f])
                + gain[:, f * cols : (f + 1) * cols]
            )
        return at

    for q, dx in offsets:
        for cc in range(nc):
            zz, xx = partner(q, dx)
            k = q * nx + dx
            at = analyse(cc, xx, zz)
            for f in range(3):
                remote(result.at[at, f], out_hbm.at[:, f, my_row], b_send.at[cc, k, f], b_recv.at[c, k, f],
                       device(zz, xx, cc, y)).start()
    at = analyse(other_c, x, z)
    for f in range(3):
        remote(result.at[at, f], out_hbm.at[:, f, my_row], b_send.at[other_c, 0, f], b_recv.at[c, 0, f],
               device(z, x, other_c, y)).start()
    at = analyse(c, x, z)
    own_copies = []
    for f in range(3):
        copy = pltpu.make_async_copy(result.at[at, f], out_hbm.at[:, f, my_row], own_sem.at[f])
        copy.start()
        own_copies.append(copy)

    for copy in halo_copies:
        for half in copy:
            half.wait_send()
    for copy in list(s.values()) + list(n.values()) + inner_sends + edge_sends + [core_send]:
        copy.wait_send()
    for q, dx in offsets:
        for cc in range(nc):
            k = q * nx + dx
            zz, xx = partner(q, dx)
            row = row_of(cc, xx, zz)
            for f in range(3):
                copy = remote(result.at[0, f], out_hbm.at[:, f, row], b_send.at[cc, k, f], b_recv.at[cc, k, f],
                              device(zz, xx, cc, y))
                copy.wait_send()
                copy.wait_recv()
    for f in range(3):
        copy = remote(result.at[0, f], out_hbm.at[:, f, row_of(other_c, x, z)], b_send.at[other_c, 0, f],
                      b_recv.at[other_c, 0, f], device(z, x, other_c, y))
        copy.wait_send()
        copy.wait_recv()
    for copy in own_copies:
        copy.wait()


def with_halo(cells, sides, width):
    for axis, dim in sides:
        count = lax.axis_size(axis)
        head = lax.slice_in_dim(cells, 0, width, axis=dim)
        tail = lax.slice_in_dim(cells, cells.shape[dim] - width, cells.shape[dim], axis=dim)
        cells = jnp.concatenate(
            [
                lax.ppermute(tail, axis, [(i, (i + 1) % count) for i in range(count)]),
                cells,
                lax.ppermute(head, axis, [((i + 1) % count, i) for i in range(count)]),
            ],
            axis=dim,
        )
    return cells


def lax_friedrichs(state):
    depth = state[:, 0]
    east = state[:, 1]
    north = state[:, 2]
    press = 0.5 * gravity * depth * depth
    flux_x = jnp.stack([east, east * east / depth + press, east * north / depth], 1)
    flux_y = jnp.stack([north, east * north / depth, north * north / depth + press], 1)
    inner = state[:, :, 1:-1]
    average = 0.25 * (
        state[:, :, 2:] + state[:, :, :-2] + jnp.roll(inner, 1, 3) + jnp.roll(inner, -1, 3)
    )
    middle = flux_x[:, :, 1:-1]
    return (
        average
        - 0.5 * courant * (jnp.roll(middle, -1, 3) - jnp.roll(middle, 1, 3))
        - 0.5 * courant * (flux_y[:, :, 2:] - flux_y[:, :, :-2])
    )


def product(left, right):
    return jnp.dot(left, right, precision=lax.Precision.HIGHEST, preferred_element_type=jnp.float32)


def plain(
    prior_fields,
    measured_point_location,
    measured_depths,
    inverse_noise_deviation,
    sample_noise_draw,
    sample_line_labels,
):
    dispersion_multiplier = math.sqrt(widen_dispersion / (sample_noise_draw.shape[0] - 1))
    propagated_fields = prior_fields
    for step in range(STEPS):
        padded = with_halo(propagated_fields, (("run", 2),), 1)
        propagated_fields = lax_friedrichs(padded)
    members = propagated_fields.shape[0]
    depth_flat = propagated_fields[:, 0].reshape(
        members, propagated_fields.shape[2] * propagated_fields.shape[3]
    )
    sampled = inverse_noise_deviation[None, :] * jnp.take(
        depth_flat, measured_point_location, axis=1
    )
    innovation = (
        inverse_noise_deviation[None, :] * measured_depths[None, :]
        - sampled
        + jnp.take(sample_noise_draw, sample_line_labels, axis=0)
    )
    all_sampled, all_innov = (
        lax.all_gather(sampled, ("role", "grp"), axis=0, tiled=True),
        lax.all_gather(innovation, ("role", "grp"), axis=0, tiled=True),
    )
    spread = dispersion_multiplier * (all_sampled - jnp.mean(all_sampled, axis=0, keepdims=True))
    first = lax.axis_index(("role", "grp")) * members
    own_spread = lax.dynamic_slice_in_dim(spread, first, members, 0)
    own_innov = lax.dynamic_slice_in_dim(all_innov, first, members, 0)
    gram_rows, cross_rows = (
        lax.psum_scatter(product(own_spread, spread.T), "run", scatter_dimension=0, tiled=True),
        lax.psum_scatter(product(own_innov, spread.T), "run", scatter_dimension=0, tiled=True),
    )
    gram = lax.all_gather(gram_rows, ("role", "grp", "run"), axis=0, tiled=True)
    upper = 1.0 + jnp.sqrt(jnp.sum(gram * gram))
    theta = (upper + 1.0) / 2.0
    delta = (upper - 1.0) / 2.0
    sigma = theta / delta
    rho = 1.0 / sigma
    residual = cross_rows
    direction = residual / theta
    linear_solution = direction
    for turn in range(CHEB - 1):
        residual = residual - direction - product(direction, gram)
        rho_next = 1.0 / (2.0 * sigma - rho)
        direction = rho_next * rho * direction + 2.0 * rho_next / delta * residual
        linear_solution = linear_solution + direction
        rho = rho_next
    posterior_coefficients = lax.all_gather(
        linear_solution, ("role", "grp", "run"), axis=0, tiled=True
    )
    ensemble_combination = (
        math.sqrt(widen_dispersion) * jnp.eye(posterior_coefficients.shape[0], dtype=jnp.float32)
        + dispersion_multiplier * posterior_coefficients
    )
    strip_slab = lax.all_to_all(
        propagated_fields, ("role", "grp"), split_axis=2, concat_axis=0, tiled=True
    )
    array_shape = strip_slab.shape
    flat = strip_slab.reshape(array_shape[0], array_shape[1] * array_shape[2] * array_shape[3])
    center = jnp.mean(flat, axis=0, keepdims=True)
    updated = (center + product(ensemble_combination, flat - center)).reshape(array_shape)
    return lax.all_to_all(updated, ("role", "grp"), split_axis=0, concat_axis=2, tiled=True)


def fused(
    dims,
    prior_fields,
    measured_point_location,
    measured_depths,
    inverse_noise_deviation,
    sample_noise_draw,
    sample_line_labels,
):
    nz, nx, nc, ny = dims
    members, _, rows, cols = prior_fields.shape
    obs = measured_point_location.shape[0]
    every = ny * obs
    group = nz * nx * nc
    slab = (group, 3, members, cols)
    gathered = (nc, ny, nx, nz, members, obs)
    total = group * members
    dma = pltpu.SemaphoreType.DMA
    vmem = pl.BlockSpec(memory_space=pltpu.VMEM)
    anywhere = pl.BlockSpec(memory_space=pl.ANY)
    hops = 19
    return pl.pallas_call(
        functools.partial(kernel, dims),
        out_shape=jax.ShapeDtypeStruct(prior_fields.shape, jnp.float32),
        in_specs=[anywhere, vmem, vmem, vmem, anywhere, pl.BlockSpec(memory_space=pltpu.SMEM)],
        out_specs=anywhere,
        scratch_shapes=[
            pltpu.VMEM((rows, 3, members, cols), jnp.float32),
            pltpu.VMEM(sample_noise_draw.shape, jnp.float32),
            pltpu.VMEM((2, STEPS, 3, members, cols), jnp.float32),
            pltpu.VMEM((rows, 3, members, cols), jnp.float32),
            pltpu.VMEM(slab, jnp.float32),
            pltpu.VMEM(slab, jnp.float32),
            pltpu.VMEM(gathered, jnp.float32),
            pltpu.VMEM(gathered, jnp.float32),
            pltpu.VMEM((every, total), jnp.bfloat16),
            pltpu.VMEM((every, total), jnp.bfloat16),
            pltpu.VMEM((4, every, every), jnp.float32),
            dma((rows, 3)),
            dma,
            dma((2 * CHUNKS,)),
            dma((2 * CHUNKS,)),
            dma((hops,)),
            dma((hops,)),
            dma((hops,)),
            dma((hops,)),
            dma((nc, nz * nx)),
            dma((nc, nz * nx)),
            dma((nc, nz * nx, 3)),
            dma((nc, nz * nx, 3)),
            dma((3,)),
            pltpu.SemaphoreType.REGULAR,
            pltpu.SemaphoreType.REGULAR,
        ],
        compiler_params=pltpu.CompilerParams(
            collective_id=0, has_side_effects=True, vmem_limit_bytes=60 * 1024 * 1024
        ),
        name="analysis_kernel",
    )(
        prior_fields,
        measured_point_location[None, :],
        measured_depths[None, :],
        inverse_noise_deviation[None, :],
        sample_noise_draw,
        sample_line_labels,
    )


def shards(shape, *args):
    nz, grp, ny = shape["role"], shape["grp"], shape["run"]
    members, _, rows, cols = args[0].shape
    fits = (
        grp == 4
        and ny == 2
        and nz == 4
        and rows == nz * grp
        and rows == 4 * STEPS
        and CHEB == 8
        and members % (CHUNKS * TILE) == 0
        and cols == 128
        and args[1].shape[0] * ny <= 512
    )
    if fits:
        return fused((nz, 2, 2, ny), *args)
    return plain(*args)


def solution(mesh):
    placed = (
        P(("role", "grp"), None, "run", None),
        P("run"),
        P("run"),
        P("run"),
        P(None, "run"),
        P(("role", "grp")),
    )
    return jax.shard_map(
        functools.partial(shards, dict(mesh.shape)),
        mesh=mesh,
        in_specs=placed,
        out_specs=P(("role", "grp"), None, "run", None),
        check_vma=False,
    )
```

```python
import functools
import math

import jax
import jax.numpy as jnp
from jax import lax
from jax.experimental import pallas as pl
from jax.experimental.pallas import tpu as pltpu
from jax.sharding import PartitionSpec as P

STEPS = 4
CHEB = 8
PARTS = (3, 3, 1, 1)
PIECES = 8
TILE = 8
FIRST = (0, 1, 2, 6, 4, 5)
SECOND = (3,)
THIRD = (7, 8)
FOURTH = ()

gravity = 1.0
courant = 0.35
widen_dispersion = 1.1

MESH = pl.DeviceIdType.MESH


def advance(fields):
    depth, east, north = fields
    half = 0.5 * courant
    inverse = 1.0 / depth
    press = 0.5 * gravity * depth * depth
    speed_x = east * inverse
    speed_y = north * inverse
    mixed = east * speed_y
    flux_x = (east, east * speed_x + press, mixed)
    flux_y = (north, mixed, north * speed_y + press)
    rows = depth.shape[0]
    out = []
    for q, fx, fy in zip(fields, flux_x, flux_y):
        quarter = 0.25 * q
        mid = quarter[1:-1]
        kx = half * fx[1:-1]
        sides = pltpu.roll(mid - kx, q.shape[2] - 1, 2) + pltpu.roll(mid + kx, 1, 2)
        up = (quarter - half * fy)[2:]
        down = (quarter + half * fy)[: rows - 2]
        out.append(sides + up + down)
    return tuple(out)


def halves(value):
    high = value.astype(jnp.bfloat16)
    return high, (value - high.astype(jnp.float32)).astype(jnp.bfloat16)


def dot(left, right, dims=((1,), (0,))):
    return lax.dot_general(left, right, (dims, ((), ())), preferred_element_type=jnp.float32)


def dot3(left, right, dims=((1,), (0,))):
    (lh, ll), (rh, rl) = left, right
    return dot(lh, rh, dims) + (dot(lh, rl, dims) + dot(ll, rh, dims))


def kernel(
    dims,
    x_hbm, loc_ref, depth_ref, inv_ref, draw_hbm, label_ref,
    out_hbm,
    prior, draw, halo, stepped, everyone, result, sampled, noise,
    st_hi, st_lo, basis,
    load_sem, draw_sem, halo_send, halo_recv, s_send, s_recv, n_send, n_recv,
    f_send, f_recv, b_send, b_recv, own_sem, plane, full,
):
    nz, nx, nc, ny = dims
    z = lax.axis_index("role")
    grp = lax.axis_index("grp")
    y = lax.axis_index("run")
    x = grp // nc
    c = grp % nc
    rows, _, members, cols = prior.shape
    obs = loc_ref.shape[1]
    total = nz * nx * nc * members
    width = STEPS

    def device(zz, xx, cc, yy):
        return (zz, xx * nc + cc, yy)

    def flat(cc, xx, zz):
        return (cc * nx + xx) * nz + zz

    def row_of(cc, xx, zz):
        return lax.rem((nc - 1 - cc) * nx * nz + width + xx * nz + zz, rows)

    me = flat(c, x, z)
    my_row = row_of(c, x, z)
    other_x = lax.rem(x + 1, nx)
    other_y = lax.rem(y + 1, ny)
    other_c = lax.rem(c + 1, nc)
    z_far = lax.rem(z + 2, nz)
    z_near = z + 1 - 2 * lax.rem(z, 2)
    z_cross = lax.rem(z_near + 2, nz)

    zs = [z, z_near, z_far, z_cross]
    offsets = [(2, 0), (3, 0), (2, 1), (3, 1), (1, 0), (1, 1), (0, 1)]

    def partner(q, dx):
        return zs[q], lax.rem(x + dx, nx)

    barrier = pltpu.get_barrier_semaphore()
    targets = [device(*partner(q, dx), 1, y) for q, dx in offsets]
    targets += [device(z, x, other_c, y), device(z, x, 0, other_y)]
    for target in targets:
        pl.semaphore_signal(barrier, inc=1, device_id=target, device_id_type=MESH)

    edge_rows = list(range(width)) + list(range(rows - width, rows))
    loads = {}
    for r in edge_rows + list(range(width, rows - width)):
        for f in range(3):
            loads[r, f] = pltpu.make_async_copy(x_hbm.at[:, f, r], prior.at[r, f], load_sem.at[r, f])
            loads[r, f].start()
    draw_copy = pltpu.make_async_copy(draw_hbm, draw, draw_sem)
    draw_copy.start()
    for r in edge_rows:
        for f in range(3):
            loads[r, f].wait()

    @pl.when(c == 0)
    def _():
        pl.semaphore_wait(barrier, 3)
        pl.semaphore_signal(plane, inc=1, device_id=device(z, x, 1, y), device_id_type=MESH)

    @pl.when(c == 1)
    def _():
        pl.semaphore_wait(plane, 1)

    def remote(src, dst, send, recv, target):
        return pltpu.make_async_remote_copy(
            src_ref=src, dst_ref=dst, send_sem=send, recv_sem=recv, device_id=target, device_id_type=MESH
        )

    first_of = [sum(PARTS[:k]) * members // sum(PARTS) for k in range(len(PARTS) + 1)]
    halo_copies = []
    for k in range(len(PARTS)):
        part = pl.ds(first_of[k], first_of[k + 1] - first_of[k])
        pair = (
            remote(prior.at[pl.ds(rows - width, width), :, part], halo.at[0, :, :, part],
                   halo_send.at[2 * k], halo_recv.at[2 * k], device(z, x, c, other_y)),
            remote(prior.at[pl.ds(0, width), :, part], halo.at[1, :, :, part],
                   halo_send.at[2 * k + 1], halo_recv.at[2 * k + 1], device(z, x, c, other_y)),
        )
        for copy in pair:
            copy.start()
        halo_copies.append(pair)

    for r in range(width, rows - width):
        for f in range(3):
            loads[r, f].wait()
    scale = inv_ref[...]
    base = scale * depth_ref[...]
    draw_copy.wait()

    def line(i, carry):
        for j in range(TILE):
            at = i * TILE + j
            noise[c, y, x, z, pl.ds(at, 1)] = base + draw[pl.ds(label_ref[at], 1)]
        return carry

    lax.fori_loop(0, members // TILE, line, 0)

    def inner(t, carry):
        at = pl.ds(pl.multiple_of(t * TILE, TILE), TILE)
        fields = tuple(prior[:, f, at] for f in range(3))
        for step in range(STEPS):
            fields = advance(fields)
        for f in range(3):
            stepped[width : rows - width, f, at] = fields[f]
        return carry

    lax.fori_loop(0, members // TILE, inner, 0)

    @pl.when(c == 1)
    def _():
        pl.semaphore_wait(barrier, nc * len(offsets) + 1)
        pl.semaphore_signal(full, inc=1, device_id=device(z, x, 0, y), device_id_type=MESH)

    @pl.when(c == 0)
    def _():
        pl.semaphore_wait(full, 1)

    def sender(cc, q, dx):
        zz, xx = partner(q, dx)
        k = q * nx + dx
        return remote(stepped.at[row_of(cc, xx, zz)], everyone.at[me], f_send.at[cc, k], f_recv.at[c, k],
                      device(zz, xx, cc, y))

    inner_sends = [sender(1, q, dx) for q, dx in offsets]
    edge_sends = [sender(0, q, dx) for q, dx in offsets]
    core_send = remote(stepped.at[row_of(other_c, x, z)], everyone.at[me], f_send.at[other_c, 0], f_recv.at[c, 0],
                       device(z, x, other_c, y))
    def gather(buf, send, recv):
        def hop(i, src, target):
            return remote(src, src, send.at[i], recv.at[i], target)

        out = {
            "far": hop(0, buf.at[c, y, x, z], device(z_far, x, c, y)),
            "near": hop(1, buf.at[c, y, x, z], device(z_near, x, c, y)),
            "relay": hop(2, buf.at[c, y, x, z_far], device(z_near, x, c, y)),
            "c0": hop(19, buf.at[c, y, x], device(z, x, other_c, y)),
            "c1": hop(20, buf.at[c, y, other_x], device(z, x, other_c, y)),
            "c2": hop(21, buf.at[c, other_y, x], device(z, x, other_c, y)),
            "c3": hop(22, buf.at[c, other_y, other_x], device(z, x, other_c, y)),
        }
        for q in range(nz):
            block = buf.at[c, y, x, zs[q]]
            out["x", q] = hop(3 + q, block, device(z, other_x, c, y))
            out["y", q] = hop(7 + q, block, device(z, x, c, other_y))
            out["w", q] = hop(11 + q, buf.at[c, y, other_x, zs[q]], device(z, x, c, other_y))
            out["v", q] = hop(15 + q, buf.at[c, other_y, x, zs[q]], device(z, other_x, c, y))
        return out

    begun = []

    def start(g, *names):
        for name in names:
            g[name].start()
            begun.append(g[name])

    def arrive(g, *names):
        for name in names:
            g[name].wait_recv()

    s = gather(sampled, s_send, s_recv)
    n = gather(noise, n_send, n_recv)
    start(n, "far", "near", ("x", 0), ("y", 0))
    for i in FIRST:
        inner_sends[i].start()

    loc = loc_ref[...]
    lanes = lax.broadcasted_iota(jnp.int32, (2 * cols, obs), 0)

    def pick(r, acc):
        hot = jnp.where(loc - r * cols == lanes, 1.0, 0.0).astype(jnp.bfloat16)
        depth = jnp.concatenate([stepped[r, 0], stepped[r + 1, 0]], 1)
        d1 = depth.astype(jnp.bfloat16)
        rest = depth - d1.astype(jnp.float32)
        d2 = rest.astype(jnp.bfloat16)
        d3 = (rest - d2.astype(jnp.float32)).astype(jnp.bfloat16)
        return acc + (dot(d1, hot) + (dot(d2, hot) + dot(d3, hot)))

    picked = jnp.zeros((members, obs), jnp.float32)
    for r in range(width, rows - width, 2):
        picked = pick(r, picked)

    arrive(n, "far")
    start(n, "relay", ("x", 2), ("y", 2))

    for k in range(len(PARTS)):
        for copy in halo_copies[k]:
            copy.wait_recv()

        def edge(t, carry):
            at = pl.ds(pl.multiple_of(t * TILE, TILE), TILE)
            for side in range(2):
                low, high = (0, 2 * width) if side == 0 else (rows - 2 * width, rows)
                fields = []
                for f in range(3):
                    own = prior[low:high, f, at]
                    fields.append(jnp.concatenate([halo[0, :, f, at], own] if side == 0 else [own, halo[1, :, f, at]], 0))
                for step in range(STEPS):
                    fields = advance(fields)
                first = 0 if side == 0 else rows - width
                for f in range(3):
                    stepped[first : first + width, f, at] = fields[f]
            return carry

        lax.fori_loop(first_of[k] // TILE, first_of[k + 1] // TILE, edge, 0)

    for r in list(range(0, width, 2)) + list(range(rows - width, rows, 2)):
        picked = pick(r, picked)
    sampled[c, y, x, z] = scale * picked
    start(s, "far", "near", ("x", 0), ("y", 0))
    for i in SECOND:
        (inner_sends + edge_sends)[i].start()
    core_send.start()
    arrive(n, "near", "relay")
    start(n, ("x", 1), ("y", 1), ("x", 3), ("y", 3))
    everyone[me] = stepped[my_row]
    arrive(s, "far")
    start(s, "relay", ("x", 2), ("y", 2))
    for i in THIRD:
        (inner_sends + edge_sends)[i].start()
    arrive(s, "near")
    start(s, ("x", 1), ("y", 1))
    arrive(s, "relay")
    start(s, ("x", 3), ("y", 3), "c0")
    for i in FOURTH:
        (inner_sends + edge_sends)[i].start()
    for q in (0, 2, 1, 3):
        arrive(s, ("x", q))
        start(s, ("w", q))
        arrive(n, ("y", q))
        start(n, ("v", q))
    start(s, "c1")
    for i, copy in enumerate(inner_sends + edge_sends):
        if i not in FIRST + SECOND + THIRD + FOURTH:
            copy.start()
    start(n, "c0", "c2")
    arrive(s, *[("y", q) for q in range(nz)])
    start(s, "c2")
    arrive(n, *[("x", q) for q in range(nz)])
    start(n, "c1")

    dispersion = math.sqrt(widen_dispersion / (total - 1))

    def spread(yy, at):
        block = sampled[:, yy].reshape(total, obs)
        value = dispersion * (block - jnp.sum(block, axis=0, keepdims=True) * (1.0 / total))
        hi, lo = halves(value.T)
        st_hi[at : at + obs] = hi
        st_lo[at : at + obs] = lo
        return st_hi[at : at + obs], st_lo[at : at + obs]

    def square(value):
        return jnp.sum(jnp.sum(value * value, axis=1, keepdims=True), axis=0, keepdims=True)

    nt = ((1,), (1,))
    every = ny * obs
    arrive(s, "c0", "c1")
    own = spread(y, 0)
    near_block = dot3(own, own, nt)
    basis[0, :obs, :obs] = near_block
    norm = square(near_block)
    arrive(s, *[("w", q) for q in range(nz)])
    start(s, "c3")
    arrive(s, "c2", "c3")
    other = spread(other_y, obs)
    far_block = dot3(other, other, nt)
    basis[0, obs:, obs:] = far_block
    mixed_block = dot3(own, other, nt)
    basis[0, :obs, obs:] = mixed_block
    basis[0, obs:, :obs] = mixed_block.T
    upper = 1.0 + jnp.sqrt(norm + square(far_block) + 2.0 * square(mixed_block))
    theta = (upper + 1.0) / 2.0
    delta = (upper - 1.0) / 2.0
    sigma = theta / delta
    rho = [1.0 / sigma]
    lead = [1.0 / theta]
    fade = rho[0]
    for turn in range(1, CHEB):
        rho.append(1.0 / (2.0 * sigma - rho[-1]))
        lead.append(2.0 * rho[-1] / delta * fade)
        fade = fade * rho[-1]
    weight = [None] * CHEB
    tail = jnp.ones_like(theta)
    for turn in reversed(range(CHEB)):
        weight[turn] = lead[turn] * tail
        tail = 1.0 + rho[turn] * rho[turn - 1] * tail
    eye = jnp.where(
        lax.broadcasted_iota(jnp.int32, (every, every), 0) == lax.broadcasted_iota(jnp.int32, (every, every), 1),
        1.0, 0.0,
    )
    t1 = eye - basis[0] * (1.0 / delta)
    basis[0] = t1
    h1 = halves(t1)
    t2 = 2.0 * dot3(h1, h1) - eye
    basis[1] = t2
    h2 = halves(t2)
    t3 = 2.0 * dot3(h1, h2) - basis[0]
    basis[2] = t3
    t4 = 2.0 * dot3(h2, h2) - eye
    upper_part = weight[5] * basis[0] + weight[6] * basis[1] + weight[7] * basis[2]
    lower_part = (
        weight[0] * eye
        + (weight[1] - weight[7]) * basis[0]
        + (weight[2] - weight[6]) * basis[1]
        + (weight[3] - weight[5]) * basis[2]
        + weight[4] * t4
    )
    basis[3] = dispersion * (lower_part + 2.0 * dot3(halves(t4), halves(upper_part)))

    for q, dx in offsets:
        for cc in range(nc):
            k = q * nx + dx
            zz, xx = partner(q, dx)
            remote(stepped.at[0], everyone.at[flat(cc, xx, zz)], f_send.at[0, k], f_recv.at[cc, k],
                   device(zz, xx, cc, y)).wait_recv()
    remote(stepped.at[0], everyone.at[flat(other_c, x, z)], f_send.at[0, 0], f_recv.at[other_c, 0],
           device(z, x, other_c, y)).wait_recv()

    center = []
    devs = []
    for f in range(3):
        values = everyone[:, f].reshape(total, cols)
        mean = jnp.sum(values, axis=0, keepdims=True) * (1.0 / total)
        center.append(mean)
        devs.append(values - mean)
    cross = dot3((st_hi[...], st_lo[...]), halves(jnp.concatenate(devs, 1)))
    whi, wlo = halves(dot3(halves(basis[3]), halves(cross)))

    arrive(n, *[("v", q) for q in range(nz)])
    start(n, "c3")
    arrive(n, "c0", "c1", "c2", "c3")

    def analyse(cc, xx, zz):
        at = flat(cc, xx, zz)
        innov = jnp.concatenate([noise[cc, yy, xx, zz] - sampled[cc, yy, xx, zz] for yy in (y, other_y)], 1)
        gain = dot3(halves(innov), (whi, wlo))
        for f in range(3):
            result[at, f] = (
                center[f]
                + math.sqrt(widen_dispersion) * (everyone[at, f] - center[f])
                + gain[:, f * cols : (f + 1) * cols]
            )
        return at

    for q, dx in offsets:
        for cc in range(nc):
            zz, xx = partner(q, dx)
            k = q * nx + dx
            at = analyse(cc, xx, zz)
            for f in range(3):
                remote(result.at[at, f], out_hbm.at[:, f, my_row], b_send.at[cc, k, f], b_recv.at[c, k, f],
                       device(zz, xx, cc, y)).start()
    at = analyse(other_c, x, z)
    for f in range(3):
        remote(result.at[at, f], out_hbm.at[:, f, my_row], b_send.at[other_c, 0, f], b_recv.at[c, 0, f],
               device(z, x, other_c, y)).start()
    at = analyse(c, x, z)
    own_copies = []
    for f in range(3):
        copy = pltpu.make_async_copy(result.at[at, f], out_hbm.at[:, f, my_row], own_sem.at[f])
        copy.start()
        own_copies.append(copy)

    for copy in halo_copies:
        for half in copy:
            half.wait_send()
    for copy in begun + inner_sends + edge_sends + [core_send]:
        copy.wait_send()
    for q, dx in offsets:
        for cc in range(nc):
            k = q * nx + dx
            zz, xx = partner(q, dx)
            row = row_of(cc, xx, zz)
            for f in range(3):
                copy = remote(result.at[0, f], out_hbm.at[:, f, row], b_send.at[cc, k, f], b_recv.at[cc, k, f],
                              device(zz, xx, cc, y))
                copy.wait_send()
                copy.wait_recv()
    for f in range(3):
        copy = remote(result.at[0, f], out_hbm.at[:, f, row_of(other_c, x, z)], b_send.at[other_c, 0, f],
                      b_recv.at[other_c, 0, f], device(z, x, other_c, y))
        copy.wait_send()
        copy.wait_recv()
    for copy in own_copies:
        copy.wait()


def with_halo(cells, sides, width):
    for axis, dim in sides:
        count = lax.axis_size(axis)
        head = lax.slice_in_dim(cells, 0, width, axis=dim)
        tail = lax.slice_in_dim(cells, cells.shape[dim] - width, cells.shape[dim], axis=dim)
        cells = jnp.concatenate(
            [
                lax.ppermute(tail, axis, [(i, (i + 1) % count) for i in range(count)]),
                cells,
                lax.ppermute(head, axis, [((i + 1) % count, i) for i in range(count)]),
            ],
            axis=dim,
        )
    return cells


def lax_friedrichs(state):
    depth = state[:, 0]
    east = state[:, 1]
    north = state[:, 2]
    press = 0.5 * gravity * depth * depth
    flux_x = jnp.stack([east, east * east / depth + press, east * north / depth], 1)
    flux_y = jnp.stack([north, east * north / depth, north * north / depth + press], 1)
    inner = state[:, :, 1:-1]
    average = 0.25 * (
        state[:, :, 2:] + state[:, :, :-2] + jnp.roll(inner, 1, 3) + jnp.roll(inner, -1, 3)
    )
    middle = flux_x[:, :, 1:-1]
    return (
        average
        - 0.5 * courant * (jnp.roll(middle, -1, 3) - jnp.roll(middle, 1, 3))
        - 0.5 * courant * (flux_y[:, :, 2:] - flux_y[:, :, :-2])
    )


def product(left, right):
    return jnp.dot(left, right, precision=lax.Precision.HIGHEST, preferred_element_type=jnp.float32)


def plain(
    prior_fields,
    measured_point_location,
    measured_depths,
    inverse_noise_deviation,
    sample_noise_draw,
    sample_line_labels,
):
    dispersion_multiplier = math.sqrt(widen_dispersion / (sample_noise_draw.shape[0] - 1))
    propagated_fields = prior_fields
    for step in range(STEPS):
        padded = with_halo(propagated_fields, (("run", 2),), 1)
        propagated_fields = lax_friedrichs(padded)
    members = propagated_fields.shape[0]
    depth_flat = propagated_fields[:, 0].reshape(
        members, propagated_fields.shape[2] * propagated_fields.shape[3]
    )
    sampled = inverse_noise_deviation[None, :] * jnp.take(
        depth_flat, measured_point_location, axis=1
    )
    innovation = (
        inverse_noise_deviation[None, :] * measured_depths[None, :]
        - sampled
        + jnp.take(sample_noise_draw, sample_line_labels, axis=0)
    )
    all_sampled, all_innov = (
        lax.all_gather(sampled, ("role", "grp"), axis=0, tiled=True),
        lax.all_gather(innovation, ("role", "grp"), axis=0, tiled=True),
    )
    spread = dispersion_multiplier * (all_sampled - jnp.mean(all_sampled, axis=0, keepdims=True))
    first = lax.axis_index(("role", "grp")) * members
    own_spread = lax.dynamic_slice_in_dim(spread, first, members, 0)
    own_innov = lax.dynamic_slice_in_dim(all_innov, first, members, 0)
    gram_rows, cross_rows = (
        lax.psum_scatter(product(own_spread, spread.T), "run", scatter_dimension=0, tiled=True),
        lax.psum_scatter(product(own_innov, spread.T), "run", scatter_dimension=0, tiled=True),
    )
    gram = lax.all_gather(gram_rows, ("role", "grp", "run"), axis=0, tiled=True)
    upper = 1.0 + jnp.sqrt(jnp.sum(gram * gram))
    theta = (upper + 1.0) / 2.0
    delta = (upper - 1.0) / 2.0
    sigma = theta / delta
    rho = 1.0 / sigma
    residual = cross_rows
    direction = residual / theta
    linear_solution = direction
    for turn in range(CHEB - 1):
        residual = residual - direction - product(direction, gram)
        rho_next = 1.0 / (2.0 * sigma - rho)
        direction = rho_next * rho * direction + 2.0 * rho_next / delta * residual
        linear_solution = linear_solution + direction
        rho = rho_next
    posterior_coefficients = lax.all_gather(
        linear_solution, ("role", "grp", "run"), axis=0, tiled=True
    )
    ensemble_combination = (
        math.sqrt(widen_dispersion) * jnp.eye(posterior_coefficients.shape[0], dtype=jnp.float32)
        + dispersion_multiplier * posterior_coefficients
    )
    strip_slab = lax.all_to_all(
        propagated_fields, ("role", "grp"), split_axis=2, concat_axis=0, tiled=True
    )
    array_shape = strip_slab.shape
    flat = strip_slab.reshape(array_shape[0], array_shape[1] * array_shape[2] * array_shape[3])
    center = jnp.mean(flat, axis=0, keepdims=True)
    updated = (center + product(ensemble_combination, flat - center)).reshape(array_shape)
    return lax.all_to_all(updated, ("role", "grp"), split_axis=0, concat_axis=2, tiled=True)


def pass_on(src, dst, held, load_sem, store_sem):
    per = src.shape[0] // PIECES
    loads, stores = [], []
    for i in range(PIECES):
        at = pl.ds(i * per, per)
        loads.append(pltpu.make_async_copy(src.at[at], held.at[at], load_sem.at[i]))
        stores.append(pltpu.make_async_copy(held.at[at], dst.at[at], store_sem.at[i]))
        loads[-1].start()
    for load, store in zip(loads, stores):
        load.wait()
        store.start()
    for store in stores:
        store.wait()


def hand_over(values):
    anywhere = pl.BlockSpec(memory_space=pl.ANY)
    return pl.pallas_call(
        pass_on,
        out_shape=jax.ShapeDtypeStruct(values.shape, values.dtype),
        in_specs=[anywhere],
        out_specs=anywhere,
        scratch_shapes=[
            pltpu.VMEM(values.shape, values.dtype),
            pltpu.SemaphoreType.DMA((PIECES,)),
            pltpu.SemaphoreType.DMA((PIECES,)),
        ],
        name="hand_over",
    )(values)


def fused(
    dims,
    prior_fields,
    measured_point_location,
    measured_depths,
    inverse_noise_deviation,
    sample_noise_draw,
    sample_line_labels,
):
    nz, nx, nc, ny = dims
    members, _, rows, cols = prior_fields.shape
    obs = measured_point_location.shape[0]
    every = ny * obs
    group = nz * nx * nc
    slab = (group, 3, members, cols)
    gathered = (nc, ny, nx, nz, members, obs)
    total = group * members
    dma = pltpu.SemaphoreType.DMA
    vmem = pl.BlockSpec(memory_space=pltpu.VMEM)
    anywhere = pl.BlockSpec(memory_space=pl.ANY)
    hops = 23
    out = pl.pallas_call(
        functools.partial(kernel, dims),
        out_shape=jax.ShapeDtypeStruct(prior_fields.shape, jnp.float32),
        in_specs=[anywhere, vmem, vmem, vmem, anywhere, pl.BlockSpec(memory_space=pltpu.SMEM)],
        out_specs=anywhere,
        scratch_shapes=[
            pltpu.VMEM((rows, 3, members, cols), jnp.float32),
            pltpu.VMEM(sample_noise_draw.shape, jnp.float32),
            pltpu.VMEM((2, STEPS, 3, members, cols), jnp.float32),
            pltpu.VMEM((rows, 3, members, cols), jnp.float32),
            pltpu.VMEM(slab, jnp.float32),
            pltpu.VMEM(slab, jnp.float32),
            pltpu.VMEM(gathered, jnp.float32),
            pltpu.VMEM(gathered, jnp.float32),
            pltpu.VMEM((every, total), jnp.bfloat16),
            pltpu.VMEM((every, total), jnp.bfloat16),
            pltpu.VMEM((4, every, every), jnp.float32),
            dma((rows, 3)),
            dma,
            dma((2 * len(PARTS),)),
            dma((2 * len(PARTS),)),
            dma((hops,)),
            dma((hops,)),
            dma((hops,)),
            dma((hops,)),
            dma((nc, nz * nx)),
            dma((nc, nz * nx)),
            dma((nc, nz * nx, 3)),
            dma((nc, nz * nx, 3)),
            dma((3,)),
            pltpu.SemaphoreType.REGULAR,
            pltpu.SemaphoreType.REGULAR,
        ],
        compiler_params=pltpu.CompilerParams(
            collective_id=0, has_side_effects=True, vmem_limit_bytes=60 * 1024 * 1024
        ),
        name="analysis_kernel",
    )(
        prior_fields,
        measured_point_location[None, :],
        measured_depths[None, :],
        inverse_noise_deviation[None, :],
        sample_noise_draw,
        sample_line_labels,
    )
    return hand_over(out)


def shards(shape, *args):
    nz, grp, ny = shape["role"], shape["grp"], shape["run"]
    members, _, rows, cols = args[0].shape
    fits = (
        grp == 4
        and ny == 2
        and nz == 4
        and rows == nz * grp
        and rows == 4 * STEPS
        and CHEB == 8
        and members % (sum(PARTS) * TILE) == 0
        and cols == 128
        and args[1].shape[0] * ny <= 512
    )
    if fits:
        return fused((nz, 2, 2, ny), *args)
    return plain(*args)


def solution(mesh):
    placed = (
        P(("role", "grp"), None, "run", None),
        P("run"),
        P("run"),
        P("run"),
        P(None, "run"),
        P(("role", "grp")),
    )
    return jax.shard_map(
        functools.partial(shards, dict(mesh.shape)),
        mesh=mesh,
        in_specs=placed,
        out_specs=P(("role", "grp"), None, "run", None),
        check_vma=False,
    )
```

```python
import functools
import math

import jax
import jax.numpy as jnp
from jax import lax
from jax.experimental import pallas as pl
from jax.experimental.pallas import tpu as pltpu
from jax.sharding import PartitionSpec as P

STEPS = 4
CHEB = 8
PARTS = (3, 3, 1, 1)
PIECES = 4
TILE = 8
FIRST = (0, 1, 2, 6, 4, 5)
SECOND = (3,)
THIRD = (7, 8, 11)
FOURTH = ()

gravity = 1.0
courant = 0.35
widen_dispersion = 1.1

MESH = pl.DeviceIdType.MESH


def advance(fields):
    depth, east, north = fields
    half = 0.5 * courant
    inverse = 1.0 / depth
    press = 0.5 * gravity * depth * depth
    speed_x = east * inverse
    speed_y = north * inverse
    mixed = east * speed_y
    flux_x = (east, east * speed_x + press, mixed)
    flux_y = (north, mixed, north * speed_y + press)
    rows = depth.shape[0]
    out = []
    for q, fx, fy in zip(fields, flux_x, flux_y):
        quarter = 0.25 * q
        mid = quarter[1:-1]
        kx = half * fx[1:-1]
        sides = pltpu.roll(mid - kx, q.shape[2] - 1, 2) + pltpu.roll(mid + kx, 1, 2)
        up = (quarter - half * fy)[2:]
        down = (quarter + half * fy)[: rows - 2]
        out.append(sides + up + down)
    return tuple(out)


def halves(value):
    high = value.astype(jnp.bfloat16)
    return high, (value - high.astype(jnp.float32)).astype(jnp.bfloat16)


def dot(left, right, dims=((1,), (0,))):
    return lax.dot_general(left, right, (dims, ((), ())), preferred_element_type=jnp.float32)


def dot3(left, right, dims=((1,), (0,))):
    (lh, ll), (rh, rl) = left, right
    return dot(lh, rh, dims) + (dot(lh, rl, dims) + dot(ll, rh, dims))


def kernel(
    dims,
    x_hbm, loc_ref, depth_ref, inv_ref, draw_hbm, label_ref,
    out_hbm,
    prior, draw, halo, stepped, everyone, result, sampled, noise,
    st_hi, st_lo, basis,
    load_sem, draw_sem, halo_send, halo_recv, s_send, s_recv, n_send, n_recv,
    f_send, f_recv, b_send, b_recv, own_sem, plane, full,
):
    nz, nx, nc, ny = dims
    z = lax.axis_index("role")
    grp = lax.axis_index("grp")
    y = lax.axis_index("run")
    x = grp // nc
    c = grp % nc
    rows, _, members, cols = prior.shape
    obs = loc_ref.shape[1]
    total = nz * nx * nc * members
    width = STEPS

    def device(zz, xx, cc, yy):
        return (zz, xx * nc + cc, yy)

    def flat(cc, xx, zz):
        return (cc * nx + xx) * nz + zz

    def row_of(cc, xx, zz):
        return lax.rem((nc - 1 - cc) * nx * nz + width + xx * nz + zz, rows)

    me = flat(c, x, z)
    my_row = row_of(c, x, z)
    other_x = lax.rem(x + 1, nx)
    other_y = lax.rem(y + 1, ny)
    other_c = lax.rem(c + 1, nc)
    z_far = lax.rem(z + 2, nz)
    z_near = z + 1 - 2 * lax.rem(z, 2)
    z_cross = lax.rem(z_near + 2, nz)

    zs = [z, z_near, z_far, z_cross]
    offsets = [(2, 0), (3, 0), (2, 1), (3, 1), (1, 0), (1, 1), (0, 1)]

    def partner(q, dx):
        return zs[q], lax.rem(x + dx, nx)

    barrier = pltpu.get_barrier_semaphore()
    targets = [device(*partner(q, dx), 1, y) for q, dx in offsets]
    targets += [device(z, x, other_c, y), device(z, x, 0, other_y)]
    for target in targets:
        pl.semaphore_signal(barrier, inc=1, device_id=target, device_id_type=MESH)

    edge_rows = list(range(width)) + list(range(rows - width, rows))
    loads = {}
    for r in edge_rows + list(range(width, rows - width)):
        for f in range(3):
            loads[r, f] = pltpu.make_async_copy(x_hbm.at[:, f, r], prior.at[r, f], load_sem.at[r, f])
            loads[r, f].start()
    draw_copy = pltpu.make_async_copy(draw_hbm, draw, draw_sem)
    draw_copy.start()
    for r in edge_rows:
        for f in range(3):
            loads[r, f].wait()

    @pl.when(c == 0)
    def _():
        pl.semaphore_wait(barrier, 3)
        pl.semaphore_signal(plane, inc=1, device_id=device(z, x, 1, y), device_id_type=MESH)

    @pl.when(c == 1)
    def _():
        pl.semaphore_wait(plane, 1)

    def remote(src, dst, send, recv, target):
        return pltpu.make_async_remote_copy(
            src_ref=src, dst_ref=dst, send_sem=send, recv_sem=recv, device_id=target, device_id_type=MESH
        )

    first_of = [sum(PARTS[:k]) * members // sum(PARTS) for k in range(len(PARTS) + 1)]
    halo_copies = []
    for k in range(len(PARTS)):
        part = pl.ds(first_of[k], first_of[k + 1] - first_of[k])
        pair = (
            remote(prior.at[pl.ds(rows - width, width), :, part], halo.at[0, :, :, part],
                   halo_send.at[2 * k], halo_recv.at[2 * k], device(z, x, c, other_y)),
            remote(prior.at[pl.ds(0, width), :, part], halo.at[1, :, :, part],
                   halo_send.at[2 * k + 1], halo_recv.at[2 * k + 1], device(z, x, c, other_y)),
        )
        for copy in pair:
            copy.start()
        halo_copies.append(pair)

    for r in range(width, rows - width):
        for f in range(3):
            loads[r, f].wait()
    scale = inv_ref[...]
    base = scale * depth_ref[...]
    draw_copy.wait()

    def line(i, carry):
        for j in range(TILE):
            at = i * TILE + j
            noise[c, y, x, z, pl.ds(at, 1)] = base + draw[pl.ds(label_ref[at], 1)]
        return carry

    lax.fori_loop(0, members // TILE, line, 0)

    def inner(t, carry):
        at = pl.ds(pl.multiple_of(t * TILE, TILE), TILE)
        fields = tuple(prior[:, f, at] for f in range(3))
        for step in range(STEPS):
            fields = advance(fields)
        for f in range(3):
            stepped[width : rows - width, f, at] = fields[f]
        return carry

    tiles = members // TILE
    lax.fori_loop(0, tiles // 2, inner, 0)

    @pl.when(c == 1)
    def _():
        pl.semaphore_wait(barrier, nc * len(offsets) + 1)
        pl.semaphore_signal(full, inc=1, device_id=device(z, x, 0, y), device_id_type=MESH)

    lax.fori_loop(tiles // 2, tiles, inner, 0)

    @pl.when(c == 0)
    def _():
        pl.semaphore_wait(full, 1)

    def sender(cc, q, dx):
        zz, xx = partner(q, dx)
        k = q * nx + dx
        return remote(stepped.at[row_of(cc, xx, zz)], everyone.at[me], f_send.at[cc, k], f_recv.at[c, k],
                      device(zz, xx, cc, y))

    inner_sends = [sender(1, q, dx) for q, dx in offsets]
    edge_sends = [sender(0, q, dx) for q, dx in offsets]
    core_send = remote(stepped.at[row_of(other_c, x, z)], everyone.at[me], f_send.at[other_c, 0], f_recv.at[c, 0],
                       device(z, x, other_c, y))
    def gather(buf, send, recv):
        def hop(i, src, target):
            return remote(src, src, send.at[i], recv.at[i], target)

        out = {
            "far": hop(0, buf.at[c, y, x, z], device(z_far, x, c, y)),
            "near": hop(1, buf.at[c, y, x, z], device(z_near, x, c, y)),
            "relay": hop(2, buf.at[c, y, x, z_far], device(z_near, x, c, y)),
            "c0": hop(19, buf.at[c, y, x], device(z, x, other_c, y)),
            "c1": hop(20, buf.at[c, y, other_x], device(z, x, other_c, y)),
            "c2": hop(21, buf.at[c, other_y, x], device(z, x, other_c, y)),
            "c3": hop(22, buf.at[c, other_y, other_x], device(z, x, other_c, y)),
        }
        for q in range(nz):
            block = buf.at[c, y, x, zs[q]]
            out["x", q] = hop(3 + q, block, device(z, other_x, c, y))
            out["y", q] = hop(7 + q, block, device(z, x, c, other_y))
            out["w", q] = hop(11 + q, buf.at[c, y, other_x, zs[q]], device(z, x, c, other_y))
            out["v", q] = hop(15 + q, buf.at[c, other_y, x, zs[q]], device(z, other_x, c, y))
        return out

    begun = []

    def start(g, *names):
        for name in names:
            g[name].start()
            begun.append(g[name])

    def arrive(g, *names):
        for name in names:
            g[name].wait_recv()

    s = gather(sampled, s_send, s_recv)
    n = gather(noise, n_send, n_recv)
    start(n, "far", "near", ("x", 0), ("y", 0))
    for i in FIRST:
        inner_sends[i].start()

    loc = loc_ref[...]
    lanes = lax.broadcasted_iota(jnp.int32, (2 * cols, obs), 0)

    def pick(r, acc):
        hot = jnp.where(loc - r * cols == lanes, 1.0, 0.0).astype(jnp.bfloat16)
        depth = jnp.concatenate([stepped[r, 0], stepped[r + 1, 0]], 1)
        d1 = depth.astype(jnp.bfloat16)
        rest = depth - d1.astype(jnp.float32)
        d2 = rest.astype(jnp.bfloat16)
        d3 = (rest - d2.astype(jnp.float32)).astype(jnp.bfloat16)
        return acc + (dot(d1, hot) + (dot(d2, hot) + dot(d3, hot)))

    picked = jnp.zeros((members, obs), jnp.float32)
    for r in range(width, rows - width, 2):
        picked = pick(r, picked)

    arrive(n, "far")
    start(n, "relay", ("x", 2), ("y", 2))

    for k in range(len(PARTS)):
        for copy in halo_copies[k]:
            copy.wait_recv()

        def edge(t, carry):
            at = pl.ds(pl.multiple_of(t * TILE, TILE), TILE)
            for side in range(2):
                low, high = (0, 2 * width) if side == 0 else (rows - 2 * width, rows)
                fields = []
                for f in range(3):
                    own = prior[low:high, f, at]
                    fields.append(jnp.concatenate([halo[0, :, f, at], own] if side == 0 else [own, halo[1, :, f, at]], 0))
                for step in range(STEPS):
                    fields = advance(fields)
                first = 0 if side == 0 else rows - width
                for f in range(3):
                    stepped[first : first + width, f, at] = fields[f]
            return carry

        lax.fori_loop(first_of[k] // TILE, first_of[k + 1] // TILE, edge, 0)

    for r in list(range(0, width, 2)) + list(range(rows - width, rows, 2)):
        picked = pick(r, picked)
    sampled[c, y, x, z] = scale * picked
    start(s, "far", "near", ("x", 0), ("y", 0))
    for i in SECOND:
        (inner_sends + edge_sends)[i].start()
    core_send.start()
    arrive(n, "near", "relay")
    start(n, ("x", 1), ("y", 1), ("x", 3), ("y", 3))
    everyone[me] = stepped[my_row]
    arrive(s, "far")
    start(s, "relay", ("x", 2), ("y", 2))
    for i in THIRD:
        (inner_sends + edge_sends)[i].start()
    arrive(s, "near")
    start(s, ("x", 1), ("y", 1))
    arrive(s, "relay")
    start(s, ("x", 3), ("y", 3), "c0")
    for i in FOURTH:
        (inner_sends + edge_sends)[i].start()
    for q in (0, 2, 1, 3):
        arrive(s, ("x", q))
        start(s, ("w", q))
        arrive(n, ("y", q))
        start(n, ("v", q))
    start(s, "c1")
    for i, copy in enumerate(inner_sends + edge_sends):
        if i not in FIRST + SECOND + THIRD + FOURTH:
            copy.start()
    start(n, "c0", "c2")
    arrive(s, *[("y", q) for q in range(nz)])
    start(s, "c2")
    arrive(n, *[("x", q) for q in range(nz)])
    start(n, "c1")

    dispersion = math.sqrt(widen_dispersion / (total - 1))

    def spread(yy, at):
        block = sampled[:, yy].reshape(total, obs)
        value = dispersion * (block - jnp.sum(block, axis=0, keepdims=True) * (1.0 / total))
        hi, lo = halves(value.T)
        st_hi[at : at + obs] = hi
        st_lo[at : at + obs] = lo
        return st_hi[at : at + obs], st_lo[at : at + obs]

    def square(value):
        return jnp.sum(jnp.sum(value * value, axis=1, keepdims=True), axis=0, keepdims=True)

    nt = ((1,), (1,))
    every = ny * obs
    arrive(s, "c0", "c1")
    own = spread(y, 0)
    near_block = dot3(own, own, nt)
    basis[0, :obs, :obs] = near_block
    norm = square(near_block)
    arrive(s, *[("w", q) for q in range(nz)])
    start(s, "c3")
    arrive(s, "c2", "c3")
    other = spread(other_y, obs)
    far_block = dot3(other, other, nt)
    basis[0, obs:, obs:] = far_block
    mixed_block = dot3(own, other, nt)
    basis[0, :obs, obs:] = mixed_block
    basis[0, obs:, :obs] = mixed_block.T
    upper = 1.0 + jnp.sqrt(norm + square(far_block) + 2.0 * square(mixed_block))
    theta = (upper + 1.0) / 2.0
    delta = (upper - 1.0) / 2.0
    sigma = theta / delta
    rho = [1.0 / sigma]
    lead = [1.0 / theta]
    fade = rho[0]
    for turn in range(1, CHEB):
        rho.append(1.0 / (2.0 * sigma - rho[-1]))
        lead.append(2.0 * rho[-1] / delta * fade)
        fade = fade * rho[-1]
    weight = [None] * CHEB
    tail = jnp.ones_like(theta)
    for turn in reversed(range(CHEB)):
        weight[turn] = lead[turn] * tail
        tail = 1.0 + rho[turn] * rho[turn - 1] * tail
    eye = jnp.where(
        lax.broadcasted_iota(jnp.int32, (every, every), 0) == lax.broadcasted_iota(jnp.int32, (every, every), 1),
        1.0, 0.0,
    )
    t1 = eye - basis[0] * (1.0 / delta)
    basis[0] = t1
    h1 = halves(t1)
    t2 = 2.0 * dot3(h1, h1) - eye
    basis[1] = t2
    h2 = halves(t2)
    t3 = 2.0 * dot3(h1, h2) - basis[0]
    basis[2] = t3
    t4 = 2.0 * dot3(h2, h2) - eye
    upper_part = weight[5] * basis[0] + weight[6] * basis[1] + weight[7] * basis[2]
    lower_part = (
        weight[0] * eye
        + (weight[1] - weight[7]) * basis[0]
        + (weight[2] - weight[6]) * basis[1]
        + (weight[3] - weight[5]) * basis[2]
        + weight[4] * t4
    )
    basis[3] = dispersion * (lower_part + 2.0 * dot3(halves(t4), halves(upper_part)))

    arrive(n, *[("v", q) for q in range(nz)])
    start(n, "c3")

    for q, dx in offsets:
        for cc in range(nc):
            k = q * nx + dx
            zz, xx = partner(q, dx)
            remote(stepped.at[0], everyone.at[flat(cc, xx, zz)], f_send.at[0, k], f_recv.at[cc, k],
                   device(zz, xx, cc, y)).wait_recv()
    remote(stepped.at[0], everyone.at[flat(other_c, x, z)], f_send.at[0, 0], f_recv.at[other_c, 0],
           device(z, x, other_c, y)).wait_recv()

    center = []
    devs = []
    for f in range(3):
        values = everyone[:, f].reshape(total, cols)
        mean = jnp.sum(values, axis=0, keepdims=True) * (1.0 / total)
        center.append(mean)
        devs.append(values - mean)
    cross = dot3((st_hi[...], st_lo[...]), halves(jnp.concatenate(devs, 1)))
    whi, wlo = halves(dot3(halves(basis[3]), halves(cross)))

    arrive(n, "c0", "c1", "c2", "c3")

    def analyse(cc, xx, zz):
        at = flat(cc, xx, zz)
        innov = jnp.concatenate([noise[cc, yy, xx, zz] - sampled[cc, yy, xx, zz] for yy in (y, other_y)], 1)
        gain = dot3(halves(innov), (whi, wlo))
        for f in range(3):
            result[at, f] = (
                center[f]
                + math.sqrt(widen_dispersion) * (everyone[at, f] - center[f])
                + gain[:, f * cols : (f + 1) * cols]
            )
        return at

    for q, dx in offsets:
        for cc in range(nc):
            zz, xx = partner(q, dx)
            k = q * nx + dx
            at = analyse(cc, xx, zz)
            for f in range(3):
                remote(result.at[at, f], out_hbm.at[:, f, my_row], b_send.at[cc, k, f], b_recv.at[c, k, f],
                       device(zz, xx, cc, y)).start()
    at = analyse(other_c, x, z)
    for f in range(3):
        remote(result.at[at, f], out_hbm.at[:, f, my_row], b_send.at[other_c, 0, f], b_recv.at[c, 0, f],
               device(z, x, other_c, y)).start()
    at = analyse(c, x, z)
    own_copies = []
    for f in range(3):
        copy = pltpu.make_async_copy(result.at[at, f], out_hbm.at[:, f, my_row], own_sem.at[f])
        copy.start()
        own_copies.append(copy)

    for copy in halo_copies:
        for half in copy:
            half.wait_send()
    for copy in begun + inner_sends + edge_sends + [core_send]:
        copy.wait_send()
    incoming = [
        remote(result.at[0, f], out_hbm.at[:, f, row_of(other_c, x, z)], b_send.at[other_c, 0, f],
               b_recv.at[other_c, 0, f], device(z, x, other_c, y))
        for f in range(3)
    ]
    for q, dx in reversed(offsets):
        for cc in range(nc):
            k = q * nx + dx
            zz, xx = partner(q, dx)
            row = row_of(cc, xx, zz)
            for f in range(3):
                incoming.append(
                    remote(result.at[0, f], out_hbm.at[:, f, row], b_send.at[cc, k, f], b_recv.at[cc, k, f],
                           device(zz, xx, cc, y))
                )
    for copy in own_copies:
        copy.wait()
    for copy in incoming:
        copy.wait_send()
    for copy in incoming:
        copy.wait_recv()


def with_halo(cells, sides, width):
    for axis, dim in sides:
        count = lax.axis_size(axis)
        head = lax.slice_in_dim(cells, 0, width, axis=dim)
        tail = lax.slice_in_dim(cells, cells.shape[dim] - width, cells.shape[dim], axis=dim)
        cells = jnp.concatenate(
            [
                lax.ppermute(tail, axis, [(i, (i + 1) % count) for i in range(count)]),
                cells,
                lax.ppermute(head, axis, [((i + 1) % count, i) for i in range(count)]),
            ],
            axis=dim,
        )
    return cells


def lax_friedrichs(state):
    depth = state[:, 0]
    east = state[:, 1]
    north = state[:, 2]
    press = 0.5 * gravity * depth * depth
    flux_x = jnp.stack([east, east * east / depth + press, east * north / depth], 1)
    flux_y = jnp.stack([north, east * north / depth, north * north / depth + press], 1)
    inner = state[:, :, 1:-1]
    average = 0.25 * (
        state[:, :, 2:] + state[:, :, :-2] + jnp.roll(inner, 1, 3) + jnp.roll(inner, -1, 3)
    )
    middle = flux_x[:, :, 1:-1]
    return (
        average
        - 0.5 * courant * (jnp.roll(middle, -1, 3) - jnp.roll(middle, 1, 3))
        - 0.5 * courant * (flux_y[:, :, 2:] - flux_y[:, :, :-2])
    )


def product(left, right):
    return jnp.dot(left, right, precision=lax.Precision.HIGHEST, preferred_element_type=jnp.float32)


def plain(
    prior_fields,
    measured_point_location,
    measured_depths,
    inverse_noise_deviation,
    sample_noise_draw,
    sample_line_labels,
):
    dispersion_multiplier = math.sqrt(widen_dispersion / (sample_noise_draw.shape[0] - 1))
    propagated_fields = prior_fields
    for step in range(STEPS):
        padded = with_halo(propagated_fields, (("run", 2),), 1)
        propagated_fields = lax_friedrichs(padded)
    members = propagated_fields.shape[0]
    depth_flat = propagated_fields[:, 0].reshape(
        members, propagated_fields.shape[2] * propagated_fields.shape[3]
    )
    sampled = inverse_noise_deviation[None, :] * jnp.take(
        depth_flat, measured_point_location, axis=1
    )
    innovation = (
        inverse_noise_deviation[None, :] * measured_depths[None, :]
        - sampled
        + jnp.take(sample_noise_draw, sample_line_labels, axis=0)
    )
    all_sampled, all_innov = (
        lax.all_gather(sampled, ("role", "grp"), axis=0, tiled=True),
        lax.all_gather(innovation, ("role", "grp"), axis=0, tiled=True),
    )
    spread = dispersion_multiplier * (all_sampled - jnp.mean(all_sampled, axis=0, keepdims=True))
    first = lax.axis_index(("role", "grp")) * members
    own_spread = lax.dynamic_slice_in_dim(spread, first, members, 0)
    own_innov = lax.dynamic_slice_in_dim(all_innov, first, members, 0)
    gram_rows, cross_rows = (
        lax.psum_scatter(product(own_spread, spread.T), "run", scatter_dimension=0, tiled=True),
        lax.psum_scatter(product(own_innov, spread.T), "run", scatter_dimension=0, tiled=True),
    )
    gram = lax.all_gather(gram_rows, ("role", "grp", "run"), axis=0, tiled=True)
    upper = 1.0 + jnp.sqrt(jnp.sum(gram * gram))
    theta = (upper + 1.0) / 2.0
    delta = (upper - 1.0) / 2.0
    sigma = theta / delta
    rho = 1.0 / sigma
    residual = cross_rows
    direction = residual / theta
    linear_solution = direction
    for turn in range(CHEB - 1):
        residual = residual - direction - product(direction, gram)
        rho_next = 1.0 / (2.0 * sigma - rho)
        direction = rho_next * rho * direction + 2.0 * rho_next / delta * residual
        linear_solution = linear_solution + direction
        rho = rho_next
    posterior_coefficients = lax.all_gather(
        linear_solution, ("role", "grp", "run"), axis=0, tiled=True
    )
    ensemble_combination = (
        math.sqrt(widen_dispersion) * jnp.eye(posterior_coefficients.shape[0], dtype=jnp.float32)
        + dispersion_multiplier * posterior_coefficients
    )
    strip_slab = lax.all_to_all(
        propagated_fields, ("role", "grp"), split_axis=2, concat_axis=0, tiled=True
    )
    array_shape = strip_slab.shape
    flat = strip_slab.reshape(array_shape[0], array_shape[1] * array_shape[2] * array_shape[3])
    center = jnp.mean(flat, axis=0, keepdims=True)
    updated = (center + product(ensemble_combination, flat - center)).reshape(array_shape)
    return lax.all_to_all(updated, ("role", "grp"), split_axis=0, concat_axis=2, tiled=True)


def pass_on(src, dst, held, load_sem, store_sem):
    per = src.shape[0] // PIECES
    loads, stores = [], []
    for i in range(PIECES):
        at = pl.ds(i * per, per)
        loads.append(pltpu.make_async_copy(src.at[at], held.at[at], load_sem.at[i]))
        stores.append(pltpu.make_async_copy(held.at[at], dst.at[at], store_sem.at[i]))
        loads[-1].start()
    for load, store in zip(loads, stores):
        load.wait()
        store.start()
    for store in stores:
        store.wait()


def hand_over(values):
    anywhere = pl.BlockSpec(memory_space=pl.ANY)
    return pl.pallas_call(
        pass_on,
        out_shape=jax.ShapeDtypeStruct(values.shape, values.dtype),
        in_specs=[anywhere],
        out_specs=anywhere,
        scratch_shapes=[
            pltpu.VMEM(values.shape, values.dtype),
            pltpu.SemaphoreType.DMA((PIECES,)),
            pltpu.SemaphoreType.DMA((PIECES,)),
        ],
        name="hand_over",
    )(values)


def fused(
    dims,
    prior_fields,
    measured_point_location,
    measured_depths,
    inverse_noise_deviation,
    sample_noise_draw,
    sample_line_labels,
):
    nz, nx, nc, ny = dims
    members, _, rows, cols = prior_fields.shape
    obs = measured_point_location.shape[0]
    every = ny * obs
    group = nz * nx * nc
    slab = (group, 3, members, cols)
    gathered = (nc, ny, nx, nz, members, obs)
    total = group * members
    dma = pltpu.SemaphoreType.DMA
    vmem = pl.BlockSpec(memory_space=pltpu.VMEM)
    anywhere = pl.BlockSpec(memory_space=pl.ANY)
    hops = 23
    out = pl.pallas_call(
        functools.partial(kernel, dims),
        out_shape=jax.ShapeDtypeStruct(prior_fields.shape, jnp.float32),
        in_specs=[anywhere, vmem, vmem, vmem, anywhere, pl.BlockSpec(memory_space=pltpu.SMEM)],
        out_specs=anywhere,
        scratch_shapes=[
            pltpu.VMEM((rows, 3, members, cols), jnp.float32),
            pltpu.VMEM(sample_noise_draw.shape, jnp.float32),
            pltpu.VMEM((2, STEPS, 3, members, cols), jnp.float32),
            pltpu.VMEM((rows, 3, members, cols), jnp.float32),
            pltpu.VMEM(slab, jnp.float32),
            pltpu.VMEM(slab, jnp.float32),
            pltpu.VMEM(gathered, jnp.float32),
            pltpu.VMEM(gathered, jnp.float32),
            pltpu.VMEM((every, total), jnp.bfloat16),
            pltpu.VMEM((every, total), jnp.bfloat16),
            pltpu.VMEM((4, every, every), jnp.float32),
            dma((rows, 3)),
            dma,
            dma((2 * len(PARTS),)),
            dma((2 * len(PARTS),)),
            dma((hops,)),
            dma((hops,)),
            dma((hops,)),
            dma((hops,)),
            dma((nc, nz * nx)),
            dma((nc, nz * nx)),
            dma((nc, nz * nx, 3)),
            dma((nc, nz * nx, 3)),
            dma((3,)),
            pltpu.SemaphoreType.REGULAR,
            pltpu.SemaphoreType.REGULAR,
        ],
        compiler_params=pltpu.CompilerParams(
            collective_id=0, has_side_effects=True, vmem_limit_bytes=60 * 1024 * 1024
        ),
        name="analysis_kernel",
    )(
        prior_fields,
        measured_point_location[None, :],
        measured_depths[None, :],
        inverse_noise_deviation[None, :],
        sample_noise_draw,
        sample_line_labels,
    )
    return hand_over(out)


def shards(shape, *args):
    nz, grp, ny = shape["role"], shape["grp"], shape["run"]
    members, _, rows, cols = args[0].shape
    fits = (
        grp == 4
        and ny == 2
        and nz == 4
        and rows == nz * grp
        and rows == 4 * STEPS
        and CHEB == 8
        and members % (sum(PARTS) * TILE) == 0
        and cols == 128
        and args[1].shape[0] * ny <= 512
    )
    if fits:
        return fused((nz, 2, 2, ny), *args)
    return plain(*args)


def solution(mesh):
    placed = (
        P(("role", "grp"), None, "run", None),
        P("run"),
        P("run"),
        P("run"),
        P(None, "run"),
        P(("role", "grp")),
    )
    return jax.shard_map(
        functools.partial(shards, dict(mesh.shape)),
        mesh=mesh,
        in_specs=placed,
        out_specs=P(("role", "grp"), None, "run", None),
        check_vma=False,
    )
```

```python
import functools
import math

import jax
import jax.numpy as jnp
from jax import lax
from jax.experimental import pallas as pl
from jax.experimental.pallas import tpu as pltpu
from jax.sharding import PartitionSpec as P

STEPS = 4
CHEB = 8
PARTS = (3, 3, 1, 1)
PIECES = 4
TILE = 8
FIRST = (0, 1, 2, 6, 4, 5)
SECOND = (3,)
THIRD = (7, 8, 11)
FOURTH = ()

gravity = 1.0
courant = 0.35
widen_dispersion = 1.1

MESH = pl.DeviceIdType.MESH


def advance(fields):
    depth, east, north = fields
    half = 0.5 * courant
    inverse = 1.0 / depth
    press = 0.5 * gravity * depth * depth
    speed_x = east * inverse
    speed_y = north * inverse
    mixed = east * speed_y
    flux_x = (east, east * speed_x + press, mixed)
    flux_y = (north, mixed, north * speed_y + press)
    rows = depth.shape[0]
    out = []
    for q, fx, fy in zip(fields, flux_x, flux_y):
        quarter = 0.25 * q
        mid = quarter[1:-1]
        kx = half * fx[1:-1]
        sides = pltpu.roll(mid - kx, q.shape[2] - 1, 2) + pltpu.roll(mid + kx, 1, 2)
        up = (quarter - half * fy)[2:]
        down = (quarter + half * fy)[: rows - 2]
        out.append(sides + up + down)
    return tuple(out)


def halves(value):
    high = value.astype(jnp.bfloat16)
    return high, (value - high.astype(jnp.float32)).astype(jnp.bfloat16)


def dot(left, right, dims=((1,), (0,))):
    return lax.dot_general(left, right, (dims, ((), ())), preferred_element_type=jnp.float32)


def dot3(left, right, dims=((1,), (0,))):
    (lh, ll), (rh, rl) = left, right
    return dot(lh, rh, dims) + (dot(lh, rl, dims) + dot(ll, rh, dims))


def kernel(
    dims,
    x_hbm, loc_ref, depth_ref, inv_ref, draw_hbm, label_ref,
    out_hbm,
    prior, draw, halo, stepped, everyone, result, sampled, noise,
    st_hi, st_lo, basis,
    load_sem, draw_sem, halo_send, halo_recv, s_send, s_recv, n_send, n_recv,
    f_send, f_recv, b_send, b_recv, own_sem, plane, full,
):
    nz, nx, nc, ny = dims
    z = lax.axis_index("role")
    grp = lax.axis_index("grp")
    y = lax.axis_index("run")
    x = grp // nc
    c = grp % nc
    rows, _, members, cols = prior.shape
    obs = loc_ref.shape[1]
    total = nz * nx * nc * members
    width = STEPS

    def device(zz, xx, cc, yy):
        return (zz, xx * nc + cc, yy)

    def flat(cc, xx, zz):
        return (cc * nx + xx) * nz + zz

    def row_of(cc, xx, zz):
        return lax.rem((nc - 1 - cc) * nx * nz + width + xx * nz + zz, rows)

    me = flat(c, x, z)
    my_row = row_of(c, x, z)
    other_x = lax.rem(x + 1, nx)
    other_y = lax.rem(y + 1, ny)
    other_c = lax.rem(c + 1, nc)
    z_far = lax.rem(z + 2, nz)
    z_near = z + 1 - 2 * lax.rem(z, 2)
    z_cross = lax.rem(z_near + 2, nz)

    zs = [z, z_near, z_far, z_cross]
    offsets = [(2, 0), (3, 0), (2, 1), (3, 1), (1, 0), (1, 1), (0, 1)]

    def partner(q, dx):
        return zs[q], lax.rem(x + dx, nx)

    barrier = pltpu.get_barrier_semaphore()
    targets = [device(*partner(q, dx), 1, y) for q, dx in offsets]
    targets += [device(z, x, other_c, y), device(z, x, 0, other_y)]
    for target in targets:
        pl.semaphore_signal(barrier, inc=1, device_id=target, device_id_type=MESH)

    edge_rows = list(range(width)) + list(range(rows - width, rows))
    loads = {}
    for r in edge_rows + list(range(width, rows - width)):
        for f in range(3):
            loads[r, f] = pltpu.make_async_copy(x_hbm.at[:, f, r], prior.at[r, f], load_sem.at[r, f])
            loads[r, f].start()
    draw_copy = pltpu.make_async_copy(draw_hbm, draw, draw_sem)
    draw_copy.start()
    for r in edge_rows:
        for f in range(3):
            loads[r, f].wait()

    @pl.when(c == 0)
    def _():
        pl.semaphore_wait(barrier, 3)
        pl.semaphore_signal(plane, inc=1, device_id=device(z, x, 1, y), device_id_type=MESH)

    @pl.when(c == 1)
    def _():
        pl.semaphore_wait(plane, 1)

    def remote(src, dst, send, recv, target):
        return pltpu.make_async_remote_copy(
            src_ref=src, dst_ref=dst, send_sem=send, recv_sem=recv, device_id=target, device_id_type=MESH
        )

    first_of = [sum(PARTS[:k]) * members // sum(PARTS) for k in range(len(PARTS) + 1)]
    halo_copies = []
    for k in range(len(PARTS)):
        part = pl.ds(first_of[k], first_of[k + 1] - first_of[k])
        pair = (
            remote(prior.at[pl.ds(rows - width, width), :, part], halo.at[0, :, :, part],
                   halo_send.at[2 * k], halo_recv.at[2 * k], device(z, x, c, other_y)),
            remote(prior.at[pl.ds(0, width), :, part], halo.at[1, :, :, part],
                   halo_send.at[2 * k + 1], halo_recv.at[2 * k + 1], device(z, x, c, other_y)),
        )
        for copy in pair:
            copy.start()
        halo_copies.append(pair)

    for r in range(width, rows - width):
        for f in range(3):
            loads[r, f].wait()
    scale = inv_ref[...]
    base = scale * depth_ref[...]
    draw_copy.wait()

    def line(i, carry):
        for j in range(TILE):
            at = i * TILE + j
            noise[c, y, x, z, pl.ds(at, 1)] = base + draw[pl.ds(label_ref[at], 1)]
        return carry

    lax.fori_loop(0, members // TILE, line, 0)

    def inner(t, carry):
        at = pl.ds(pl.multiple_of(t * TILE, TILE), TILE)
        fields = tuple(prior[:, f, at] for f in range(3))
        for step in range(STEPS):
            fields = advance(fields)
        for f in range(3):
            stepped[width : rows - width, f, at] = fields[f]
        return carry

    tiles = members // TILE
    lax.fori_loop(0, tiles // 2, inner, 0)

    @pl.when(c == 1)
    def _():
        pl.semaphore_wait(barrier, nc * len(offsets) + 1)
        pl.semaphore_signal(full, inc=1, device_id=device(z, x, 0, y), device_id_type=MESH)

    lax.fori_loop(tiles // 2, tiles, inner, 0)

    @pl.when(c == 0)
    def _():
        pl.semaphore_wait(full, 1)

    def sender(cc, q, dx):
        zz, xx = partner(q, dx)
        k = q * nx + dx
        return remote(stepped.at[row_of(cc, xx, zz)], everyone.at[me], f_send.at[cc, k], f_recv.at[c, k],
                      device(zz, xx, cc, y))

    inner_sends = [sender(1, q, dx) for q, dx in offsets]
    edge_sends = [sender(0, q, dx) for q, dx in offsets]
    core_send = remote(stepped.at[row_of(other_c, x, z)], everyone.at[me], f_send.at[other_c, 0], f_recv.at[c, 0],
                       device(z, x, other_c, y))
    def gather(buf, send, recv):
        def hop(i, src, target):
            return remote(src, src, send.at[i], recv.at[i], target)

        out = {
            "far": hop(0, buf.at[c, y, x, z], device(z_far, x, c, y)),
            "near": hop(1, buf.at[c, y, x, z], device(z_near, x, c, y)),
            "relay": hop(2, buf.at[c, y, x, z_far], device(z_near, x, c, y)),
            "c0": hop(19, buf.at[c, y, x], device(z, x, other_c, y)),
            "c1": hop(20, buf.at[c, y, other_x], device(z, x, other_c, y)),
            "c2": hop(21, buf.at[c, other_y, x], device(z, x, other_c, y)),
            "c3": hop(22, buf.at[c, other_y, other_x], device(z, x, other_c, y)),
        }
        for q in range(nz):
            block = buf.at[c, y, x, zs[q]]
            out["x", q] = hop(3 + q, block, device(z, other_x, c, y))
            out["y", q] = hop(7 + q, block, device(z, x, c, other_y))
            out["w", q] = hop(11 + q, buf.at[c, y, other_x, zs[q]], device(z, x, c, other_y))
            out["v", q] = hop(15 + q, buf.at[c, other_y, x, zs[q]], device(z, other_x, c, y))
        return out

    begun = []

    def start(g, *names):
        for name in names:
            g[name].start()
            begun.append(g[name])

    def arrive(g, *names):
        for name in names:
            g[name].wait_recv()

    s = gather(sampled, s_send, s_recv)
    n = gather(noise, n_send, n_recv)
    start(n, "far", "near", ("x", 0), ("y", 0))
    for i in FIRST:
        inner_sends[i].start()

    loc = loc_ref[...]
    lanes = lax.broadcasted_iota(jnp.int32, (2 * cols, obs), 0)

    def pick(r, acc):
        hot = jnp.where(loc - r * cols == lanes, 1.0, 0.0).astype(jnp.bfloat16)
        depth = jnp.concatenate([stepped[r, 0], stepped[r + 1, 0]], 1)
        d1 = depth.astype(jnp.bfloat16)
        rest = depth - d1.astype(jnp.float32)
        d2 = rest.astype(jnp.bfloat16)
        d3 = (rest - d2.astype(jnp.float32)).astype(jnp.bfloat16)
        return acc + (dot(d1, hot) + (dot(d2, hot) + dot(d3, hot)))

    picked = jnp.zeros((members, obs), jnp.float32)
    for r in range(width, rows - width, 2):
        picked = pick(r, picked)

    arrive(n, "far")
    start(n, "relay", ("x", 2), ("y", 2))

    for k in range(len(PARTS)):
        for copy in halo_copies[k]:
            copy.wait_recv()

        def edge(t, carry):
            at = pl.ds(pl.multiple_of(t * TILE, TILE), TILE)
            for side in range(2):
                low, high = (0, 2 * width) if side == 0 else (rows - 2 * width, rows)
                fields = []
                for f in range(3):
                    own = prior[low:high, f, at]
                    fields.append(jnp.concatenate([halo[0, :, f, at], own] if side == 0 else [own, halo[1, :, f, at]], 0))
                for step in range(STEPS):
                    fields = advance(fields)
                first = 0 if side == 0 else rows - width
                for f in range(3):
                    stepped[first : first + width, f, at] = fields[f]
            return carry

        lax.fori_loop(first_of[k] // TILE, first_of[k + 1] // TILE, edge, 0)

    for r in list(range(0, width, 2)) + list(range(rows - width, rows, 2)):
        picked = pick(r, picked)
    sampled[c, y, x, z] = scale * picked
    start(s, "far", "near", ("x", 0), ("y", 0))
    for i in SECOND:
        (inner_sends + edge_sends)[i].start()
    core_send.start()
    arrive(n, "near", "relay")
    start(n, ("x", 1), ("y", 1), ("x", 3), ("y", 3))
    everyone[me] = stepped[my_row]
    arrive(s, "far")
    start(s, "relay", ("x", 2), ("y", 2))
    for i in THIRD:
        (inner_sends + edge_sends)[i].start()
    arrive(s, "near")
    start(s, ("x", 1), ("y", 1))
    arrive(s, "relay")
    start(s, ("x", 3), ("y", 3), "c0")
    for i in FOURTH:
        (inner_sends + edge_sends)[i].start()
    for q in (0, 2, 1, 3):
        arrive(s, ("x", q))
        start(s, ("w", q))
        arrive(n, ("y", q))
        start(n, ("v", q))
    start(s, "c1")
    for i, copy in enumerate(inner_sends + edge_sends):
        if i not in FIRST + SECOND + THIRD + FOURTH:
            copy.start()
    start(n, "c0", "c2")
    arrive(s, *[("y", q) for q in range(nz)])
    start(s, "c2")
    arrive(n, *[("x", q) for q in range(nz)])
    start(n, "c1")

    dispersion = math.sqrt(widen_dispersion / (total - 1))

    def spread(yy, at):
        block = sampled[:, yy].reshape(total, obs)
        value = dispersion * (block - jnp.sum(block, axis=0, keepdims=True) * (1.0 / total))
        hi, lo = halves(value.T)
        st_hi[at : at + obs] = hi
        st_lo[at : at + obs] = lo
        return st_hi[at : at + obs], st_lo[at : at + obs]

    def square(value):
        return jnp.sum(jnp.sum(value * value, axis=1, keepdims=True), axis=0, keepdims=True)

    nt = ((1,), (1,))
    every = ny * obs
    arrive(s, "c0", "c1")
    own = spread(y, 0)
    near_block = dot3(own, own, nt)
    basis[0, :obs, :obs] = near_block
    norm = square(near_block)
    arrive(s, *[("w", q) for q in range(nz)])
    start(s, "c3")
    arrive(s, "c2", "c3")
    other = spread(other_y, obs)
    far_block = dot3(other, other, nt)
    basis[0, obs:, obs:] = far_block
    mixed_block = dot3(own, other, nt)
    basis[0, :obs, obs:] = mixed_block
    basis[0, obs:, :obs] = mixed_block.T
    upper = 1.0 + jnp.sqrt(norm + square(far_block) + 2.0 * square(mixed_block))
    theta = (upper + 1.0) / 2.0
    delta = (upper - 1.0) / 2.0
    sigma = theta / delta
    rho = [1.0 / sigma]
    lead = [1.0 / theta]
    fade = rho[0]
    for turn in range(1, CHEB):
        rho.append(1.0 / (2.0 * sigma - rho[-1]))
        lead.append(2.0 * rho[-1] / delta * fade)
        fade = fade * rho[-1]
    weight = [None] * CHEB
    tail = jnp.ones_like(theta)
    for turn in reversed(range(CHEB)):
        weight[turn] = lead[turn] * tail
        tail = 1.0 + rho[turn] * rho[turn - 1] * tail
    eye = jnp.where(
        lax.broadcasted_iota(jnp.int32, (every, every), 0) == lax.broadcasted_iota(jnp.int32, (every, every), 1),
        1.0, 0.0,
    )
    t1 = eye - basis[0] * (1.0 / delta)
    basis[0] = t1
    h1 = halves(t1)
    t2 = 2.0 * dot3(h1, h1) - eye
    basis[1] = t2
    h2 = halves(t2)
    t3 = 2.0 * dot3(h1, h2) - basis[0]
    basis[2] = t3
    t4 = 2.0 * dot3(h2, h2) - eye
    upper_part = weight[5] * basis[0] + weight[6] * basis[1] + weight[7] * basis[2]
    lower_part = (
        weight[0] * eye
        + (weight[1] - weight[7]) * basis[0]
        + (weight[2] - weight[6]) * basis[1]
        + (weight[3] - weight[5]) * basis[2]
        + weight[4] * t4
    )
    basis[3] = dispersion * (lower_part + 2.0 * dot3(halves(t4), halves(upper_part)))

    arrive(n, *[("v", q) for q in range(nz)])
    start(n, "c3")

    for q, dx in offsets:
        for cc in range(nc):
            k = q * nx + dx
            zz, xx = partner(q, dx)
            remote(stepped.at[0], everyone.at[flat(cc, xx, zz)], f_send.at[0, k], f_recv.at[cc, k],
                   device(zz, xx, cc, y)).wait_recv()
    remote(stepped.at[0], everyone.at[flat(other_c, x, z)], f_send.at[0, 0], f_recv.at[other_c, 0],
           device(z, x, other_c, y)).wait_recv()

    center = []
    devs = []
    for f in range(3):
        values = everyone[:, f].reshape(total, cols)
        mean = jnp.sum(values, axis=0, keepdims=True) * (1.0 / total)
        center.append(mean)
        devs.append(values - mean)
    cross = dot3((st_hi[...], st_lo[...]), halves(jnp.concatenate(devs, 1)))
    whi, wlo = halves(dot3(halves(basis[3]), halves(cross)))

    arrive(n, "c0", "c1", "c2", "c3")

    def analyse(cc, xx, zz):
        at = flat(cc, xx, zz)
        innov = jnp.concatenate([noise[cc, yy, xx, zz] - sampled[cc, yy, xx, zz] for yy in (y, other_y)], 1)
        gain = dot3(halves(innov), (whi, wlo))
        for f in range(3):
            result[at, f] = (
                center[f]
                + math.sqrt(widen_dispersion) * (everyone[at, f] - center[f])
                + gain[:, f * cols : (f + 1) * cols]
            )
        return at

    for q, dx in offsets:
        for cc in range(nc):
            zz, xx = partner(q, dx)
            k = q * nx + dx
            at = analyse(cc, xx, zz)
            for f in range(3):
                remote(result.at[at, f], out_hbm.at[:, f, my_row], b_send.at[cc, k], b_recv.at[c, k],
                       device(zz, xx, cc, y)).start()
    at = analyse(other_c, x, z)
    for f in range(3):
        remote(result.at[at, f], out_hbm.at[:, f, my_row], b_send.at[other_c, 0], b_recv.at[c, 0],
               device(z, x, other_c, y)).start()
    at = analyse(c, x, z)
    own_copies = []
    for f in range(3):
        copy = pltpu.make_async_copy(result.at[at, f], out_hbm.at[:, f, my_row], own_sem.at[f])
        copy.start()
        own_copies.append(copy)

    for copy in halo_copies:
        for half in copy:
            half.wait_send()
    for copy in begun + inner_sends + edge_sends + [core_send]:
        copy.wait_send()
    slab = result.at[flat(other_c, x, z)]
    incoming = [remote(slab, slab, b_send.at[other_c, 0], b_recv.at[other_c, 0], device(z, x, other_c, y))]
    for q, dx in reversed(offsets):
        for cc in range(nc):
            k = q * nx + dx
            zz, xx = partner(q, dx)
            slab = result.at[flat(cc, xx, zz)]
            incoming.append(remote(slab, slab, b_send.at[cc, k], b_recv.at[cc, k], device(zz, xx, cc, y)))
    for copy in own_copies:
        copy.wait()
    for copy in incoming:
        copy.wait_send()
    for copy in incoming:
        copy.wait_recv()


def with_halo(cells, sides, width):
    for axis, dim in sides:
        count = lax.axis_size(axis)
        head = lax.slice_in_dim(cells, 0, width, axis=dim)
        tail = lax.slice_in_dim(cells, cells.shape[dim] - width, cells.shape[dim], axis=dim)
        cells = jnp.concatenate(
            [
                lax.ppermute(tail, axis, [(i, (i + 1) % count) for i in range(count)]),
                cells,
                lax.ppermute(head, axis, [((i + 1) % count, i) for i in range(count)]),
            ],
            axis=dim,
        )
    return cells


def lax_friedrichs(state):
    depth = state[:, 0]
    east = state[:, 1]
    north = state[:, 2]
    press = 0.5 * gravity * depth * depth
    flux_x = jnp.stack([east, east * east / depth + press, east * north / depth], 1)
    flux_y = jnp.stack([north, east * north / depth, north * north / depth + press], 1)
    inner = state[:, :, 1:-1]
    average = 0.25 * (
        state[:, :, 2:] + state[:, :, :-2] + jnp.roll(inner, 1, 3) + jnp.roll(inner, -1, 3)
    )
    middle = flux_x[:, :, 1:-1]
    return (
        average
        - 0.5 * courant * (jnp.roll(middle, -1, 3) - jnp.roll(middle, 1, 3))
        - 0.5 * courant * (flux_y[:, :, 2:] - flux_y[:, :, :-2])
    )


def product(left, right):
    return jnp.dot(left, right, precision=lax.Precision.HIGHEST, preferred_element_type=jnp.float32)


def plain(
    prior_fields,
    measured_point_location,
    measured_depths,
    inverse_noise_deviation,
    sample_noise_draw,
    sample_line_labels,
):
    dispersion_multiplier = math.sqrt(widen_dispersion / (sample_noise_draw.shape[0] - 1))
    propagated_fields = prior_fields
    for step in range(STEPS):
        padded = with_halo(propagated_fields, (("run", 2),), 1)
        propagated_fields = lax_friedrichs(padded)
    members = propagated_fields.shape[0]
    depth_flat = propagated_fields[:, 0].reshape(
        members, propagated_fields.shape[2] * propagated_fields.shape[3]
    )
    sampled = inverse_noise_deviation[None, :] * jnp.take(
        depth_flat, measured_point_location, axis=1
    )
    innovation = (
        inverse_noise_deviation[None, :] * measured_depths[None, :]
        - sampled
        + jnp.take(sample_noise_draw, sample_line_labels, axis=0)
    )
    all_sampled, all_innov = (
        lax.all_gather(sampled, ("role", "grp"), axis=0, tiled=True),
        lax.all_gather(innovation, ("role", "grp"), axis=0, tiled=True),
    )
    spread = dispersion_multiplier * (all_sampled - jnp.mean(all_sampled, axis=0, keepdims=True))
    first = lax.axis_index(("role", "grp")) * members
    own_spread = lax.dynamic_slice_in_dim(spread, first, members, 0)
    own_innov = lax.dynamic_slice_in_dim(all_innov, first, members, 0)
    gram_rows, cross_rows = (
        lax.psum_scatter(product(own_spread, spread.T), "run", scatter_dimension=0, tiled=True),
        lax.psum_scatter(product(own_innov, spread.T), "run", scatter_dimension=0, tiled=True),
    )
    gram = lax.all_gather(gram_rows, ("role", "grp", "run"), axis=0, tiled=True)
    upper = 1.0 + jnp.sqrt(jnp.sum(gram * gram))
    theta = (upper + 1.0) / 2.0
    delta = (upper - 1.0) / 2.0
    sigma = theta / delta
    rho = 1.0 / sigma
    residual = cross_rows
    direction = residual / theta
    linear_solution = direction
    for turn in range(CHEB - 1):
        residual = residual - direction - product(direction, gram)
        rho_next = 1.0 / (2.0 * sigma - rho)
        direction = rho_next * rho * direction + 2.0 * rho_next / delta * residual
        linear_solution = linear_solution + direction
        rho = rho_next
    posterior_coefficients = lax.all_gather(
        linear_solution, ("role", "grp", "run"), axis=0, tiled=True
    )
    ensemble_combination = (
        math.sqrt(widen_dispersion) * jnp.eye(posterior_coefficients.shape[0], dtype=jnp.float32)
        + dispersion_multiplier * posterior_coefficients
    )
    strip_slab = lax.all_to_all(
        propagated_fields, ("role", "grp"), split_axis=2, concat_axis=0, tiled=True
    )
    array_shape = strip_slab.shape
    flat = strip_slab.reshape(array_shape[0], array_shape[1] * array_shape[2] * array_shape[3])
    center = jnp.mean(flat, axis=0, keepdims=True)
    updated = (center + product(ensemble_combination, flat - center)).reshape(array_shape)
    return lax.all_to_all(updated, ("role", "grp"), split_axis=0, concat_axis=2, tiled=True)


def pass_on(src, dst, held, load_sem, store_sem):
    per = src.shape[0] // PIECES
    loads, stores = [], []
    for i in range(PIECES):
        at = pl.ds(i * per, per)
        loads.append(pltpu.make_async_copy(src.at[at], held.at[at], load_sem.at[i]))
        stores.append(pltpu.make_async_copy(held.at[at], dst.at[at], store_sem.at[i]))
        loads[-1].start()
    for load, store in zip(loads, stores):
        load.wait()
        store.start()
    for store in stores:
        store.wait()


def hand_over(values):
    anywhere = pl.BlockSpec(memory_space=pl.ANY)
    return pl.pallas_call(
        pass_on,
        out_shape=jax.ShapeDtypeStruct(values.shape, values.dtype),
        in_specs=[anywhere],
        out_specs=anywhere,
        scratch_shapes=[
            pltpu.VMEM(values.shape, values.dtype),
            pltpu.SemaphoreType.DMA((PIECES,)),
            pltpu.SemaphoreType.DMA((PIECES,)),
        ],
        name="hand_over",
    )(values)


def fused(
    dims,
    prior_fields,
    measured_point_location,
    measured_depths,
    inverse_noise_deviation,
    sample_noise_draw,
    sample_line_labels,
):
    nz, nx, nc, ny = dims
    members, _, rows, cols = prior_fields.shape
    obs = measured_point_location.shape[0]
    every = ny * obs
    group = nz * nx * nc
    slab = (group, 3, members, cols)
    gathered = (nc, ny, nx, nz, members, obs)
    total = group * members
    dma = pltpu.SemaphoreType.DMA
    vmem = pl.BlockSpec(memory_space=pltpu.VMEM)
    anywhere = pl.BlockSpec(memory_space=pl.ANY)
    hops = 23
    out = pl.pallas_call(
        functools.partial(kernel, dims),
        out_shape=jax.ShapeDtypeStruct(prior_fields.shape, jnp.float32),
        in_specs=[anywhere, vmem, vmem, vmem, anywhere, pl.BlockSpec(memory_space=pltpu.SMEM)],
        out_specs=anywhere,
        scratch_shapes=[
            pltpu.VMEM((rows, 3, members, cols), jnp.float32),
            pltpu.VMEM(sample_noise_draw.shape, jnp.float32),
            pltpu.VMEM((2, STEPS, 3, members, cols), jnp.float32),
            pltpu.VMEM((rows, 3, members, cols), jnp.float32),
            pltpu.VMEM(slab, jnp.float32),
            pltpu.VMEM(slab, jnp.float32),
            pltpu.VMEM(gathered, jnp.float32),
            pltpu.VMEM(gathered, jnp.float32),
            pltpu.VMEM((every, total), jnp.bfloat16),
            pltpu.VMEM((every, total), jnp.bfloat16),
            pltpu.VMEM((4, every, every), jnp.float32),
            dma((rows, 3)),
            dma,
            dma((2 * len(PARTS),)),
            dma((2 * len(PARTS),)),
            dma((hops,)),
            dma((hops,)),
            dma((hops,)),
            dma((hops,)),
            dma((nc, nz * nx)),
            dma((nc, nz * nx)),
            dma((nc, nz * nx)),
            dma((nc, nz * nx)),
            dma((3,)),
            pltpu.SemaphoreType.REGULAR,
            pltpu.SemaphoreType.REGULAR,
        ],
        compiler_params=pltpu.CompilerParams(
            collective_id=0, has_side_effects=True, vmem_limit_bytes=60 * 1024 * 1024
        ),
        name="analysis_kernel",
    )(
        prior_fields,
        measured_point_location[None, :],
        measured_depths[None, :],
        inverse_noise_deviation[None, :],
        sample_noise_draw,
        sample_line_labels,
    )
    return hand_over(out)


def shards(shape, *args):
    nz, grp, ny = shape["role"], shape["grp"], shape["run"]
    members, _, rows, cols = args[0].shape
    fits = (
        grp == 4
        and ny == 2
        and nz == 4
        and rows == nz * grp
        and rows == 4 * STEPS
        and CHEB == 8
        and members % (sum(PARTS) * TILE) == 0
        and cols == 128
        and args[1].shape[0] * ny <= 512
    )
    if fits:
        return fused((nz, 2, 2, ny), *args)
    return plain(*args)


def solution(mesh):
    placed = (
        P(("role", "grp"), None, "run", None),
        P("run"),
        P("run"),
        P("run"),
        P(None, "run"),
        P(("role", "grp")),
    )
    return jax.shard_map(
        functools.partial(shards, dict(mesh.shape)),
        mesh=mesh,
        in_specs=placed,
        out_specs=P(("role", "grp"), None, "run", None),
        check_vma=False,
    )
```

```python
import functools
import math

import jax
import jax.numpy as jnp
from jax import lax
from jax.experimental import pallas as pl
from jax.experimental.pallas import tpu as pltpu
from jax.sharding import PartitionSpec as P

STEPS = 4
CHEB = 8
PARTS = (3, 3, 1, 1)
PIECES = 4
TILE = 8
FIRST = (0, 1, 2, 6, 4, 5)
SECOND = (3,)
THIRD = (7, 8, 11)
FOURTH = ()

gravity = 1.0
courant = 0.35
widen_dispersion = 1.1

MESH = pl.DeviceIdType.MESH


def advance(fields):
    depth, east, north = fields
    half = 0.5 * courant
    inverse = 1.0 / depth
    press = 0.5 * gravity * depth * depth
    speed_x = east * inverse
    speed_y = north * inverse
    mixed = east * speed_y
    flux_x = (east, east * speed_x + press, mixed)
    flux_y = (north, mixed, north * speed_y + press)
    rows = depth.shape[0]
    out = []
    for q, fx, fy in zip(fields, flux_x, flux_y):
        quarter = 0.25 * q
        mid = quarter[1:-1]
        kx = half * fx[1:-1]
        sides = pltpu.roll(mid - kx, q.shape[2] - 1, 2) + pltpu.roll(mid + kx, 1, 2)
        up = (quarter - half * fy)[2:]
        down = (quarter + half * fy)[: rows - 2]
        out.append(sides + up + down)
    return tuple(out)


def halves(value):
    high = value.astype(jnp.bfloat16)
    return high, (value - high.astype(jnp.float32)).astype(jnp.bfloat16)


def dot(left, right, dims=((1,), (0,))):
    return lax.dot_general(left, right, (dims, ((), ())), preferred_element_type=jnp.float32)


def dot3(left, right, dims=((1,), (0,))):
    (lh, ll), (rh, rl) = left, right
    return dot(lh, rh, dims) + (dot(lh, rl, dims) + dot(ll, rh, dims))


def kernel(
    dims,
    x_hbm, loc_ref, depth_ref, inv_ref, draw_hbm, label_ref,
    out_hbm,
    prior, draw, halo, stepped, everyone, result, sampled, noise,
    st_hi, st_lo, basis,
    load_sem, draw_sem, halo_send, halo_recv, s_send, s_recv, n_send, n_recv,
    f_send, f_recv, b_send, b_recv, own_sem, plane, full,
):
    nz, nx, nc, ny = dims
    z = lax.axis_index("role")
    grp = lax.axis_index("grp")
    y = lax.axis_index("run")
    x = grp // nc
    c = grp % nc
    rows, _, members, cols = prior.shape
    obs = loc_ref.shape[1]
    total = nz * nx * nc * members
    width = STEPS

    def device(zz, xx, cc, yy):
        return (zz, xx * nc + cc, yy)

    def flat(cc, xx, zz):
        return (cc * nx + xx) * nz + zz

    def row_of(cc, xx, zz):
        return lax.rem((nc - 1 - cc) * nx * nz + width + xx * nz + zz, rows)

    me = flat(c, x, z)
    my_row = row_of(c, x, z)
    other_x = lax.rem(x + 1, nx)
    other_y = lax.rem(y + 1, ny)
    other_c = lax.rem(c + 1, nc)
    z_far = lax.rem(z + 2, nz)
    z_near = z + 1 - 2 * lax.rem(z, 2)
    z_cross = lax.rem(z_near + 2, nz)

    zs = [z, z_near, z_far, z_cross]
    offsets = [(2, 0), (3, 0), (2, 1), (3, 1), (1, 0), (1, 1), (0, 1)]

    def partner(q, dx):
        return zs[q], lax.rem(x + dx, nx)

    barrier = pltpu.get_barrier_semaphore()
    targets = [device(*partner(q, dx), 1, y) for q, dx in offsets]
    targets += [device(z, x, other_c, y), device(z, x, 0, other_y)]
    for target in targets:
        pl.semaphore_signal(barrier, inc=1, device_id=target, device_id_type=MESH)

    edge_rows = list(range(width)) + list(range(rows - width, rows))
    loads = {}
    for r in edge_rows + list(range(width, rows - width)):
        for f in range(3):
            loads[r, f] = pltpu.make_async_copy(x_hbm.at[:, f, r], prior.at[r, f], load_sem.at[r, f])
            loads[r, f].start()
    draw_copy = pltpu.make_async_copy(draw_hbm, draw, draw_sem)
    draw_copy.start()
    for r in edge_rows:
        for f in range(3):
            loads[r, f].wait()

    @pl.when(c == 0)
    def _():
        pl.semaphore_wait(barrier, 3)
        pl.semaphore_signal(plane, inc=1, device_id=device(z, x, 1, y), device_id_type=MESH)

    @pl.when(c == 1)
    def _():
        pl.semaphore_wait(plane, 1)

    def remote(src, dst, send, recv, target):
        return pltpu.make_async_remote_copy(
            src_ref=src, dst_ref=dst, send_sem=send, recv_sem=recv, device_id=target, device_id_type=MESH
        )

    first_of = [sum(PARTS[:k]) * members // sum(PARTS) for k in range(len(PARTS) + 1)]
    halo_copies = []
    for k in range(len(PARTS)):
        part = pl.ds(first_of[k], first_of[k + 1] - first_of[k])
        pair = (
            remote(prior.at[pl.ds(rows - width, width), :, part], halo.at[0, :, :, part],
                   halo_send.at[2 * k], halo_recv.at[2 * k], device(z, x, c, other_y)),
            remote(prior.at[pl.ds(0, width), :, part], halo.at[1, :, :, part],
                   halo_send.at[2 * k + 1], halo_recv.at[2 * k + 1], device(z, x, c, other_y)),
        )
        for copy in pair:
            copy.start()
        halo_copies.append(pair)

    for r in range(width, rows - width):
        for f in range(3):
            loads[r, f].wait()
    scale = inv_ref[...]
    base = scale * depth_ref[...]
    draw_copy.wait()

    def line(i, carry):
        for j in range(TILE):
            at = i * TILE + j
            noise[c, y, x, z, pl.ds(at, 1)] = base + draw[pl.ds(label_ref[at], 1)]
        return carry

    lax.fori_loop(0, members // TILE, line, 0)

    def inner(t, carry):
        at = pl.ds(pl.multiple_of(t * TILE, TILE), TILE)
        fields = tuple(prior[:, f, at] for f in range(3))
        for step in range(STEPS):
            fields = advance(fields)
        for f in range(3):
            stepped[width : rows - width, f, at] = fields[f]
        return carry

    tiles = members // TILE
    lax.fori_loop(0, tiles // 2, inner, 0)

    @pl.when(c == 1)
    def _():
        pl.semaphore_wait(barrier, nc * len(offsets) + 1)
        pl.semaphore_signal(full, inc=1, device_id=device(z, x, 0, y), device_id_type=MESH)

    lax.fori_loop(tiles // 2, tiles, inner, 0)

    @pl.when(c == 0)
    def _():
        pl.semaphore_wait(full, 1)

    def sender(cc, q, dx):
        zz, xx = partner(q, dx)
        k = q * nx + dx
        return remote(stepped.at[row_of(cc, xx, zz)], everyone.at[me], f_send.at[cc, k], f_recv.at[c, k],
                      device(zz, xx, cc, y))

    inner_sends = [sender(1, q, dx) for q, dx in offsets]
    edge_sends = [sender(0, q, dx) for q, dx in offsets]
    core_send = remote(stepped.at[row_of(other_c, x, z)], everyone.at[me], f_send.at[other_c, 0], f_recv.at[c, 0],
                       device(z, x, other_c, y))
    def gather(buf, send, recv):
        def hop(i, src, target):
            return remote(src, src, send.at[i], recv.at[i], target)

        out = {
            "far": hop(0, buf.at[c, y, x, z], device(z_far, x, c, y)),
            "near": hop(1, buf.at[c, y, x, z], device(z_near, x, c, y)),
            "relay": hop(2, buf.at[c, y, x, z_far], device(z_near, x, c, y)),
            "c0": hop(19, buf.at[c, y, x], device(z, x, other_c, y)),
            "c1": hop(20, buf.at[c, y, other_x], device(z, x, other_c, y)),
            "c2": hop(21, buf.at[c, other_y, x], device(z, x, other_c, y)),
        }
        for q in range(nz):
            block = buf.at[c, y, x, zs[q]]
            out["x", q] = hop(3 + q, block, device(z, other_x, c, y))
            out["y", q] = hop(7 + q, block, device(z, x, c, other_y))
            out["w", q] = hop(11 + q, buf.at[c, y, other_x, zs[q]], device(z, x, c, other_y))
            out["k", q] = hop(23 + q, buf.at[c, other_y, other_x, zs[q]], device(z, x, other_c, y))
            out["v", q] = hop(15 + q, buf.at[c, other_y, x, zs[q]], device(z, other_x, c, y))
        return out

    begun = []

    def start(g, *names):
        for name in names:
            g[name].start()
            begun.append(g[name])

    def arrive(g, *names):
        for name in names:
            g[name].wait_recv()

    s = gather(sampled, s_send, s_recv)
    n = gather(noise, n_send, n_recv)
    start(n, "far", "near", ("x", 0), ("y", 0))
    for i in FIRST:
        inner_sends[i].start()

    loc = loc_ref[...]
    lanes = lax.broadcasted_iota(jnp.int32, (2 * cols, obs), 0)

    def pick(r, acc):
        hot = jnp.where(loc - r * cols == lanes, 1.0, 0.0).astype(jnp.bfloat16)
        depth = jnp.concatenate([stepped[r, 0], stepped[r + 1, 0]], 1)
        d1 = depth.astype(jnp.bfloat16)
        rest = depth - d1.astype(jnp.float32)
        d2 = rest.astype(jnp.bfloat16)
        d3 = (rest - d2.astype(jnp.float32)).astype(jnp.bfloat16)
        return acc + (dot(d1, hot) + (dot(d2, hot) + dot(d3, hot)))

    picked = jnp.zeros((members, obs), jnp.float32)
    for r in range(width, rows - width, 2):
        picked = pick(r, picked)

    arrive(n, "far")
    start(n, "relay", ("x", 2), ("y", 2))

    for k in range(len(PARTS)):
        for copy in halo_copies[k]:
            copy.wait_recv()

        def edge(t, carry):
            at = pl.ds(pl.multiple_of(t * TILE, TILE), TILE)
            for side in range(2):
                low, high = (0, 2 * width) if side == 0 else (rows - 2 * width, rows)
                fields = []
                for f in range(3):
                    own = prior[low:high, f, at]
                    fields.append(jnp.concatenate([halo[0, :, f, at], own] if side == 0 else [own, halo[1, :, f, at]], 0))
                for step in range(STEPS):
                    fields = advance(fields)
                first = 0 if side == 0 else rows - width
                for f in range(3):
                    stepped[first : first + width, f, at] = fields[f]
            return carry

        lax.fori_loop(first_of[k] // TILE, first_of[k + 1] // TILE, edge, 0)

    for r in list(range(0, width, 2)) + list(range(rows - width, rows, 2)):
        picked = pick(r, picked)
    sampled[c, y, x, z] = scale * picked
    start(s, "far", "near", ("x", 0), ("y", 0))
    for i in SECOND:
        (inner_sends + edge_sends)[i].start()
    core_send.start()
    arrive(n, "near", "relay")
    start(n, ("x", 1), ("y", 1), ("x", 3), ("y", 3))
    everyone[me] = stepped[my_row]
    arrive(s, "far")
    start(s, "relay", ("x", 2), ("y", 2))
    for i in THIRD:
        (inner_sends + edge_sends)[i].start()
    arrive(s, "near")
    start(s, ("x", 1), ("y", 1))
    arrive(s, "relay")
    start(s, ("x", 3), ("y", 3), "c0")
    for i in FOURTH:
        (inner_sends + edge_sends)[i].start()
    for q in (0, 2, 1, 3):
        arrive(s, ("x", q))
        start(s, ("w", q))
        arrive(n, ("y", q))
        start(n, ("v", q))
    start(s, "c1")
    for i, copy in enumerate(inner_sends + edge_sends):
        if i not in FIRST + SECOND + THIRD + FOURTH:
            copy.start()
    start(n, "c0", "c2")
    arrive(s, *[("y", q) for q in range(nz)])
    start(s, "c2")
    arrive(n, *[("x", q) for q in range(nz)])
    start(n, "c1")

    dispersion = math.sqrt(widen_dispersion / (total - 1))

    def spread(yy, at):
        block = sampled[:, yy].reshape(total, obs)
        value = dispersion * (block - jnp.sum(block, axis=0, keepdims=True) * (1.0 / total))
        hi, lo = halves(value.T)
        st_hi[at : at + obs] = hi
        st_lo[at : at + obs] = lo
        return st_hi[at : at + obs], st_lo[at : at + obs]

    def square(value):
        return jnp.sum(jnp.sum(value * value, axis=1, keepdims=True), axis=0, keepdims=True)

    nt = ((1,), (1,))
    every = ny * obs
    arrive(s, "c0", "c1")
    own = spread(y, 0)
    near_block = dot3(own, own, nt)
    basis[0, :obs, :obs] = near_block
    norm = square(near_block)
    for q in (0, 2, 1, 3):
        arrive(s, ("w", q))
        start(s, ("k", q))
    arrive(s, "c2", *[("k", q) for q in range(nz)])
    other = spread(other_y, obs)
    far_block = dot3(other, other, nt)
    basis[0, obs:, obs:] = far_block
    mixed_block = dot3(own, other, nt)
    basis[0, :obs, obs:] = mixed_block
    basis[0, obs:, :obs] = mixed_block.T
    upper = 1.0 + jnp.sqrt(norm + square(far_block) + 2.0 * square(mixed_block))
    theta = (upper + 1.0) / 2.0
    delta = (upper - 1.0) / 2.0
    sigma = theta / delta
    rho = [1.0 / sigma]
    lead = [1.0 / theta]
    fade = rho[0]
    for turn in range(1, CHEB):
        rho.append(1.0 / (2.0 * sigma - rho[-1]))
        lead.append(2.0 * rho[-1] / delta * fade)
        fade = fade * rho[-1]
    weight = [None] * CHEB
    tail = jnp.ones_like(theta)
    for turn in reversed(range(CHEB)):
        weight[turn] = lead[turn] * tail
        tail = 1.0 + rho[turn] * rho[turn - 1] * tail
    eye = jnp.where(
        lax.broadcasted_iota(jnp.int32, (every, every), 0) == lax.broadcasted_iota(jnp.int32, (every, every), 1),
        1.0, 0.0,
    )
    t1 = eye - basis[0] * (1.0 / delta)
    basis[0] = t1
    h1 = halves(t1)
    t2 = 2.0 * dot3(h1, h1) - eye
    basis[1] = t2
    h2 = halves(t2)
    t3 = 2.0 * dot3(h1, h2) - basis[0]
    basis[2] = t3
    t4 = 2.0 * dot3(h2, h2) - eye
    upper_part = weight[5] * basis[0] + weight[6] * basis[1] + weight[7] * basis[2]
    lower_part = (
        weight[0] * eye
        + (weight[1] - weight[7]) * basis[0]
        + (weight[2] - weight[6]) * basis[1]
        + (weight[3] - weight[5]) * basis[2]
        + weight[4] * t4
    )
    basis[3] = dispersion * (lower_part + 2.0 * dot3(halves(t4), halves(upper_part)))

    for q in (0, 2, 1, 3):
        arrive(n, ("v", q))
        start(n, ("k", q))

    for q, dx in offsets:
        for cc in range(nc):
            k = q * nx + dx
            zz, xx = partner(q, dx)
            remote(stepped.at[0], everyone.at[flat(cc, xx, zz)], f_send.at[0, k], f_recv.at[cc, k],
                   device(zz, xx, cc, y)).wait_recv()
    remote(stepped.at[0], everyone.at[flat(other_c, x, z)], f_send.at[0, 0], f_recv.at[other_c, 0],
           device(z, x, other_c, y)).wait_recv()

    center = []
    devs = []
    for f in range(3):
        values = everyone[:, f].reshape(total, cols)
        mean = jnp.sum(values, axis=0, keepdims=True) * (1.0 / total)
        center.append(mean)
        devs.append(values - mean)
    cross = dot3((st_hi[...], st_lo[...]), halves(jnp.concatenate(devs, 1)))
    whi, wlo = halves(dot3(halves(basis[3]), halves(cross)))

    arrive(n, "c0", "c1", "c2", *[("k", q) for q in range(nz)])

    def analyse(cc, xx, zz):
        at = flat(cc, xx, zz)
        innov = jnp.concatenate([noise[cc, yy, xx, zz] - sampled[cc, yy, xx, zz] for yy in (y, other_y)], 1)
        gain = dot3(halves(innov), (whi, wlo))
        for f in range(3):
            result[at, f] = (
                center[f]
                + math.sqrt(widen_dispersion) * (everyone[at, f] - center[f])
                + gain[:, f * cols : (f + 1) * cols]
            )
        return at

    for q, dx in offsets:
        for cc in range(nc):
            zz, xx = partner(q, dx)
            k = q * nx + dx
            at = analyse(cc, xx, zz)
            for f in range(3):
                remote(result.at[at, f], out_hbm.at[:, f, my_row], b_send.at[cc, k], b_recv.at[c, k],
                       device(zz, xx, cc, y)).start()
    at = analyse(other_c, x, z)
    for f in range(3):
        remote(result.at[at, f], out_hbm.at[:, f, my_row], b_send.at[other_c, 0], b_recv.at[c, 0],
               device(z, x, other_c, y)).start()
    at = analyse(c, x, z)
    own_copies = []
    for f in range(3):
        copy = pltpu.make_async_copy(result.at[at, f], out_hbm.at[:, f, my_row], own_sem.at[f])
        copy.start()
        own_copies.append(copy)

    for copy in halo_copies:
        for half in copy:
            half.wait_send()
    for copy in begun + inner_sends + edge_sends + [core_send]:
        copy.wait_send()
    slab = result.at[flat(other_c, x, z)]
    incoming = [remote(slab, slab, b_send.at[other_c, 0], b_recv.at[other_c, 0], device(z, x, other_c, y))]
    for q, dx in reversed(offsets):
        for cc in range(nc):
            k = q * nx + dx
            zz, xx = partner(q, dx)
            slab = result.at[flat(cc, xx, zz)]
            incoming.append(remote(slab, slab, b_send.at[cc, k], b_recv.at[cc, k], device(zz, xx, cc, y)))
    for copy in own_copies:
        copy.wait()
    for copy in incoming:
        copy.wait_send()
    for copy in incoming:
        copy.wait_recv()


def with_halo(cells, sides, width):
    for axis, dim in sides:
        count = lax.axis_size(axis)
        head = lax.slice_in_dim(cells, 0, width, axis=dim)
        tail = lax.slice_in_dim(cells, cells.shape[dim] - width, cells.shape[dim], axis=dim)
        cells = jnp.concatenate(
            [
                lax.ppermute(tail, axis, [(i, (i + 1) % count) for i in range(count)]),
                cells,
                lax.ppermute(head, axis, [((i + 1) % count, i) for i in range(count)]),
            ],
            axis=dim,
        )
    return cells


def lax_friedrichs(state):
    depth = state[:, 0]
    east = state[:, 1]
    north = state[:, 2]
    press = 0.5 * gravity * depth * depth
    flux_x = jnp.stack([east, east * east / depth + press, east * north / depth], 1)
    flux_y = jnp.stack([north, east * north / depth, north * north / depth + press], 1)
    inner = state[:, :, 1:-1]
    average = 0.25 * (
        state[:, :, 2:] + state[:, :, :-2] + jnp.roll(inner, 1, 3) + jnp.roll(inner, -1, 3)
    )
    middle = flux_x[:, :, 1:-1]
    return (
        average
        - 0.5 * courant * (jnp.roll(middle, -1, 3) - jnp.roll(middle, 1, 3))
        - 0.5 * courant * (flux_y[:, :, 2:] - flux_y[:, :, :-2])
    )


def product(left, right):
    return jnp.dot(left, right, precision=lax.Precision.HIGHEST, preferred_element_type=jnp.float32)


def plain(
    prior_fields,
    measured_point_location,
    measured_depths,
    inverse_noise_deviation,
    sample_noise_draw,
    sample_line_labels,
):
    dispersion_multiplier = math.sqrt(widen_dispersion / (sample_noise_draw.shape[0] - 1))
    propagated_fields = prior_fields
    for step in range(STEPS):
        padded = with_halo(propagated_fields, (("run", 2),), 1)
        propagated_fields = lax_friedrichs(padded)
    members = propagated_fields.shape[0]
    depth_flat = propagated_fields[:, 0].reshape(
        members, propagated_fields.shape[2] * propagated_fields.shape[3]
    )
    sampled = inverse_noise_deviation[None, :] * jnp.take(
        depth_flat, measured_point_location, axis=1
    )
    innovation = (
        inverse_noise_deviation[None, :] * measured_depths[None, :]
        - sampled
        + jnp.take(sample_noise_draw, sample_line_labels, axis=0)
    )
    all_sampled, all_innov = (
        lax.all_gather(sampled, ("role", "grp"), axis=0, tiled=True),
        lax.all_gather(innovation, ("role", "grp"), axis=0, tiled=True),
    )
    spread = dispersion_multiplier * (all_sampled - jnp.mean(all_sampled, axis=0, keepdims=True))
    first = lax.axis_index(("role", "grp")) * members
    own_spread = lax.dynamic_slice_in_dim(spread, first, members, 0)
    own_innov = lax.dynamic_slice_in_dim(all_innov, first, members, 0)
    gram_rows, cross_rows = (
        lax.psum_scatter(product(own_spread, spread.T), "run", scatter_dimension=0, tiled=True),
        lax.psum_scatter(product(own_innov, spread.T), "run", scatter_dimension=0, tiled=True),
    )
    gram = lax.all_gather(gram_rows, ("role", "grp", "run"), axis=0, tiled=True)
    upper = 1.0 + jnp.sqrt(jnp.sum(gram * gram))
    theta = (upper + 1.0) / 2.0
    delta = (upper - 1.0) / 2.0
    sigma = theta / delta
    rho = 1.0 / sigma
    residual = cross_rows
    direction = residual / theta
    linear_solution = direction
    for turn in range(CHEB - 1):
        residual = residual - direction - product(direction, gram)
        rho_next = 1.0 / (2.0 * sigma - rho)
        direction = rho_next * rho * direction + 2.0 * rho_next / delta * residual
        linear_solution = linear_solution + direction
        rho = rho_next
    posterior_coefficients = lax.all_gather(
        linear_solution, ("role", "grp", "run"), axis=0, tiled=True
    )
    ensemble_combination = (
        math.sqrt(widen_dispersion) * jnp.eye(posterior_coefficients.shape[0], dtype=jnp.float32)
        + dispersion_multiplier * posterior_coefficients
    )
    strip_slab = lax.all_to_all(
        propagated_fields, ("role", "grp"), split_axis=2, concat_axis=0, tiled=True
    )
    array_shape = strip_slab.shape
    flat = strip_slab.reshape(array_shape[0], array_shape[1] * array_shape[2] * array_shape[3])
    center = jnp.mean(flat, axis=0, keepdims=True)
    updated = (center + product(ensemble_combination, flat - center)).reshape(array_shape)
    return lax.all_to_all(updated, ("role", "grp"), split_axis=0, concat_axis=2, tiled=True)


def pass_on(src, dst, held, load_sem, store_sem):
    per = src.shape[0] // PIECES
    loads, stores = [], []
    for i in range(PIECES):
        at = pl.ds(i * per, per)
        loads.append(pltpu.make_async_copy(src.at[at], held.at[at], load_sem.at[i]))
        stores.append(pltpu.make_async_copy(held.at[at], dst.at[at], store_sem.at[i]))
        loads[-1].start()
    for load, store in zip(loads, stores):
        load.wait()
        store.start()
    for store in stores:
        store.wait()


def hand_over(values):
    anywhere = pl.BlockSpec(memory_space=pl.ANY)
    return pl.pallas_call(
        pass_on,
        out_shape=jax.ShapeDtypeStruct(values.shape, values.dtype),
        in_specs=[anywhere],
        out_specs=anywhere,
        scratch_shapes=[
            pltpu.VMEM(values.shape, values.dtype),
            pltpu.SemaphoreType.DMA((PIECES,)),
            pltpu.SemaphoreType.DMA((PIECES,)),
        ],
        name="hand_over",
    )(values)


def fused(
    dims,
    prior_fields,
    measured_point_location,
    measured_depths,
    inverse_noise_deviation,
    sample_noise_draw,
    sample_line_labels,
):
    nz, nx, nc, ny = dims
    members, _, rows, cols = prior_fields.shape
    obs = measured_point_location.shape[0]
    every = ny * obs
    group = nz * nx * nc
    slab = (group, 3, members, cols)
    gathered = (nc, ny, nx, nz, members, obs)
    total = group * members
    dma = pltpu.SemaphoreType.DMA
    vmem = pl.BlockSpec(memory_space=pltpu.VMEM)
    anywhere = pl.BlockSpec(memory_space=pl.ANY)
    hops = 27
    out = pl.pallas_call(
        functools.partial(kernel, dims),
        out_shape=jax.ShapeDtypeStruct(prior_fields.shape, jnp.float32),
        in_specs=[anywhere, vmem, vmem, vmem, anywhere, pl.BlockSpec(memory_space=pltpu.SMEM)],
        out_specs=anywhere,
        scratch_shapes=[
            pltpu.VMEM((rows, 3, members, cols), jnp.float32),
            pltpu.VMEM(sample_noise_draw.shape, jnp.float32),
            pltpu.VMEM((2, STEPS, 3, members, cols), jnp.float32),
            pltpu.VMEM((rows, 3, members, cols), jnp.float32),
            pltpu.VMEM(slab, jnp.float32),
            pltpu.VMEM(slab, jnp.float32),
            pltpu.VMEM(gathered, jnp.float32),
            pltpu.VMEM(gathered, jnp.float32),
            pltpu.VMEM((every, total), jnp.bfloat16),
            pltpu.VMEM((every, total), jnp.bfloat16),
            pltpu.VMEM((4, every, every), jnp.float32),
            dma((rows, 3)),
            dma,
            dma((2 * len(PARTS),)),
            dma((2 * len(PARTS),)),
            dma((hops,)),
            dma((hops,)),
            dma((hops,)),
            dma((hops,)),
            dma((nc, nz * nx)),
            dma((nc, nz * nx)),
            dma((nc, nz * nx)),
            dma((nc, nz * nx)),
            dma((3,)),
            pltpu.SemaphoreType.REGULAR,
            pltpu.SemaphoreType.REGULAR,
        ],
        compiler_params=pltpu.CompilerParams(
            collective_id=0, has_side_effects=True, vmem_limit_bytes=60 * 1024 * 1024
        ),
        name="analysis_kernel",
    )(
        prior_fields,
        measured_point_location[None, :],
        measured_depths[None, :],
        inverse_noise_deviation[None, :],
        sample_noise_draw,
        sample_line_labels,
    )
    return hand_over(out)


def shards(shape, *args):
    nz, grp, ny = shape["role"], shape["grp"], shape["run"]
    members, _, rows, cols = args[0].shape
    fits = (
        grp == 4
        and ny == 2
        and nz == 4
        and rows == nz * grp
        and rows == 4 * STEPS
        and CHEB == 8
        and members % (sum(PARTS) * TILE) == 0
        and cols == 128
        and args[1].shape[0] * ny <= 512
    )
    if fits:
        return fused((nz, 2, 2, ny), *args)
    return plain(*args)


def solution(mesh):
    placed = (
        P(("role", "grp"), None, "run", None),
        P("run"),
        P("run"),
        P("run"),
        P(None, "run"),
        P(("role", "grp")),
    )
    return jax.shard_map(
        functools.partial(shards, dict(mesh.shape)),
        mesh=mesh,
        in_specs=placed,
        out_specs=P(("role", "grp"), None, "run", None),
        check_vma=False,
    )
```
